32 devices in a mesh: fsdp: 16 (over z, y, x), tp: 2 (over core).
Axes of the slice: x: 2, y: 2, z: 4, core: 2. Of those that a mesh axis runs over, the one named last changes fastest.
Arguments:
- tokens: bfloat16 [2, 4096, 2048], P(None, ('fsdp', 'tp')), may hold values from -6 to 6
- seg_ids: int32 [2, 4096], P(None, 'fsdp'), may hold values from 0 to 31, never falling along the last dimension, each value on 1 to 400 neighbouring positions
- norm1_gain: bfloat16 [2048], P('fsdp'), may hold values from 0.5 to 1.5
- in_weight: bfloat16 [2048, 3, 2048], P(None, None, ('fsdp', 'tp')), may hold values from -0.125 to 0.125
- conv_weight: bfloat16 [3, 2048], P(None, ('fsdp', 'tp')), may hold values from -3.5 to 3.5
- out_weight: bfloat16 [2048, 2048], P(('fsdp', 'tp')), may hold values from -0.125 to 0.125
- norm2_gain: bfloat16 [2048], P('fsdp'), may hold values from 0.5 to 1.5
- gate_weight: bfloat16 [2048, 5632], P(None, ('fsdp', 'tp')), may hold values from -0.125 to 0.125
- up_weight: bfloat16 [2048, 5632], P(None, ('fsdp', 'tp')), may hold values from -0.125 to 0.125
- down_weight: bfloat16 [5632, 2048], P(('fsdp', 'tp')), may hold values from -0.109375 to 0.109375
- cotangent: bfloat16 [2, 4096, 2048], P(None, ('fsdp', 'tp')), may hold values from -6 to 6
Outputs:
- block_output: bfloat16 [2, 4096, 2048], P(None, ('fsdp', 'tp'))
- input_grad: bfloat16 [2, 4096, 2048], P(None, ('fsdp', 'tp'))
- norm1_grad: float32 [2048], P('fsdp')
- in_grad: float32 [2048, 3, 2048], P(None, None, ('fsdp', 'tp'))
- conv_grad: float32 [3, 2048], P(None, ('fsdp', 'tp'))
- out_grad: float32 [2048, 2048], P(('fsdp', 'tp'))
- norm2_grad: float32 [2048], P('fsdp')
- gate_grad: float32 [2048, 5632], P(None, ('fsdp', 'tp'))
- up_grad: float32 [2048, 5632], P(None, ('fsdp', 'tp'))
- down_grad: float32 [5632, 2048], P(('fsdp', 'tp'))
The draws below stay inside these ranges and needn't reach their ends.
Inputs may be any that keep to these rules, and one draw needn't show every extreme that they name: `seg_ids`: along each micro-batch's 4096 rows the ids never fall; a document spans at most 400 rows, and one spans exactly min(400, 2048).
All inputs are finite; a program needn't handle non-finite values.
Results may differ from the reference program's by a relative error of at most 0.02.
Values may be sent and summed in bfloat16 or wider, within the bound.
No kernel may reach another device: no remote copies, remote signals or barrier semaphores. Data moves between devices by JAX's collectives and lax.ppermute only.
A program may use at most 168 MiB of HBM per device.

```python
import math
import jax
import jax.numpy as jnp
import numpy as np
from jax import lax

D = 2048
FF = 5632
KERNEL = 3
SEQ_LEN = 256
MB = 2
ROWS = 4096
N_FSDP = 16


def steps_of(key, shape, shards, low, high):
    loudness = 1.0
    for position, shards_of in shards:
        steps = jax.random.uniform(jax.random.fold_in(jax.random.fold_in(key, 6), position), (shards_of,), jnp.float32, low / len(shards), high / len(shards))
        loudness = loudness * jnp.repeat(jnp.exp(steps), shape[position] // shards_of).reshape((-1,) + (1,) * (len(shape) - 1 - position))
    return loudness


def profile(number_of, total, most, slope):
    weights = [(1 << 20) // math.isqrt(grade ** slope) + 1 for grade in range(2, number_of + 1)]
    surplus, holding = total - most - (number_of - 1), [1] * (number_of - 1)
    while surplus > 0:
        candidates = [i for i in range(number_of - 1) if holding[i] < most]
        whole, left = sum([weights[i] for i in candidates]), surplus
        for i in candidates:
            more = min(most - holding[i], max(1, left * weights[i] // whole), surplus)
            holding[i] = holding[i] + more
            surplus = surplus - more
    return np.array([most] + holding)


def ragged_sizes(rng, amount, total, most, lean):
    if amount == 2:
        one = jax.random.randint(rng, (), max(1, total - most), min(most, total - 1) + 1)
        return jnp.stack([one, total - one])
    sizes = jnp.asarray(profile(amount, total, most, lean), jnp.int32)
    twos = (amount - 1) // 2
    donor, sink = sizes[1:1 + 2 * twos:2], sizes[2:2 + 2 * twos:2]
    room = jnp.minimum(donor - 1, most - sink)
    moved = jax.random.randint(jax.random.fold_in(rng, 1), (twos,), 0, 1 << 20) % (room + 1)
    sizes = sizes.at[1:1 + 2 * twos:2].set(donor - moved).at[2:2 + 2 * twos:2].set(sink + moved)
    return sizes[jax.random.permutation(jax.random.fold_in(rng, 2), amount)]


def noise(key, extent, scale, limit, shards=(), kind=jnp.bfloat16):
    values = jax.random.normal(key, extent, jnp.float32) * scale
    if len(shards) > 0:
        values = steps_of(key, extent, shards, -0.22, 0.18) * values
    return jnp.clip(values, min=-limit, max=limit).astype(kind)


def setup_inputs(seed: int = 0) -> dict:
    key_list = jax.random.split(jax.random.key(seed), 12)
    return {
        "tokens": noise(key_list[0], (MB, ROWS, D), 1.0, 6.0, ((1, 32),)),
        "seg_ids": jax.vmap(lambda own: jnp.searchsorted(jnp.cumsum(ragged_sizes(own, ROWS // 128, ROWS, min(400, ROWS // 2), 1)), jnp.arange(ROWS), side="right"))(jax.random.split(key_list[1], MB)).reshape((MB, ROWS)).astype(jnp.int32),
        "norm1_gain": jnp.clip(1.0 + 0.1 * jax.random.normal(key_list[2], (D,), jnp.float32), 0.5, 1.5).astype(jnp.bfloat16),
        "in_weight": noise(key_list[3], (D, 3, D), D ** -0.5, 0.125, ((2, 32),)),
        "conv_weight": noise(key_list[4], (KERNEL, D), 3 ** -0.5, 3.5, ((1, 32),)),
        "out_weight": noise(key_list[5], (D, D), D ** -0.5, 0.125, ((0, 32),)),
        "norm2_gain": jnp.clip(1.0 + 0.1 * jax.random.normal(key_list[6], (D,), jnp.float32), 0.5, 1.5).astype(jnp.bfloat16),
        "gate_weight": noise(key_list[7], (D, FF), D ** -0.5, 0.125, ((1, 32),)),
        "up_weight": noise(key_list[8], (D, FF), D ** -0.5, 0.125, ((1, 32),)),
        "down_weight": noise(key_list[9], (FF, D), (FF // 2) ** -0.5, 0.109375, ((0, 32),)),
        "cotangent": noise(key_list[10], (MB, ROWS, D), 1.0, 6.0, ((1, 32),)),
    }


EPS = 1e-05
HIGH = lax.Precision.HIGHEST

@jax.custom_vjp
def low(v):
    return lax.optimization_barrier(v.astype(jnp.bfloat16)).astype(jnp.float32)

@jax.custom_vjp
def low_back(v):
    return v

def low_keep(v):
    return (low(v), None)

def low_pass(kept, grad):
    return (grad,)

def back_keep(v):
    return (v, None)

def back_low(kept, grad):
    return (low(grad),)
low.defvjp(low_keep, low_pass)
low_back.defvjp(back_keep, back_low)

def rms_norm(value, gain):
    return value * lax.rsqrt(lax.optimization_barrier(jnp.mean(value * value, -1, keepdims=True)) + EPS) * gain

def shifted(value, places):
    return jnp.concatenate([jnp.zeros((places, value.shape[1]), jnp.float32), value[:-places]], 0)

def same_doc(seg_row, places):
    equal = seg_row[places:] == seg_row[:-places]
    return jnp.concatenate([jnp.zeros((places,), jnp.bool_), equal], 0)[:, None]

def short_conv(gated_in, seg_row, kernel):
    one_back = jnp.where(same_doc(seg_row, 1), shifted(gated_in, 1), 0.0)
    two_back = jnp.where(same_doc(seg_row, 2), shifted(gated_in, 2), 0.0)
    return kernel[0] * gated_in + kernel[1] * one_back + kernel[2] * two_back

def forward(seq_in, seg_row, gain_one, in_mat, conv_mat, out_mat, gain_two, gate_mat, up_mat, down_mat):
    normed = low(rms_norm(seq_in, gain_one))
    projected = low_back(jnp.einsum('td,dkc->tkc', normed, in_mat, precision=HIGH))
    gated_in = projected[:, 1] * projected[:, 2]
    conv_out = short_conv(gated_in, seg_row, conv_mat)
    mixed = low(projected[:, 0] * conv_out)
    mixer_out = low_back(jnp.dot(mixed, out_mat, precision=HIGH))
    resid = seq_in + mixer_out
    normed_two = low(rms_norm(resid, gain_two))
    gate_pre = low_back(jnp.dot(normed_two, gate_mat, precision=HIGH))
    up_pre = low_back(jnp.dot(normed_two, up_mat, precision=HIGH))
    hidden = low(jax.nn.silu(gate_pre) * up_pre)
    ffn_out = low_back(jnp.dot(hidden, down_mat, precision=HIGH))
    return resid + ffn_out

def reference(tokens, seg_ids, norm1_gain, in_weight, conv_weight, out_weight, norm2_gain, gate_weight, up_weight, down_weight, cotangent):
    seq_count = MB * N_FSDP
    sequences = tokens.astype(jnp.float32).reshape(seq_count, SEQ_LEN, D)
    cot_rows = cotangent.astype(jnp.float32).reshape(seq_count, SEQ_LEN, D)
    seg_rows = seg_ids.reshape(seq_count, SEQ_LEN)
    params = tuple((param.astype(jnp.float32) for param in (norm1_gain, in_weight, conv_weight, out_weight, norm2_gain, gate_weight, up_weight, down_weight)))

    def one_sequence(totals, scan_items):
        seq_in, seg_row, cot_row = scan_items

        def run_block(value, gain_one, in_mat, conv_mat, out_mat, gain_two, gate_mat, up_mat, down_mat):
            return forward(value, seg_row, gain_one, in_mat, conv_mat, out_mat, gain_two, gate_mat, up_mat, down_mat)
        result, pullback = jax.vjp(run_block, seq_in, *params)
        gradients = pullback(cot_row)
        totals = tuple((first + second for first, second in zip(totals, gradients[1:])))
        return (totals, (result.astype(jnp.bfloat16), gradients[0].astype(jnp.bfloat16)))
    start_totals = tuple((jnp.zeros_like(param) for param in params))
    totals, (block_rows, grad_rows) = lax.scan(one_sequence, start_totals, (sequences, seg_rows, cot_rows))
    return (block_rows.reshape(MB, ROWS, D), grad_rows.reshape(MB, ROWS, D), totals[0], totals[1], totals[2], totals[3], totals[4], totals[5], totals[6], totals[7])
```

```python
import jax
import jax.numpy as jnp
from jax import lax
from jax.sharding import PartitionSpec as P

EPS = 1e-05
RING = (0, 1, 3, 2)
PLANE = 4


def matmul(left, right):
    return jnp.dot(left, right, preferred_element_type=jnp.float32)


def times_trans(left, right):
    return lax.dot_general(
        left, right, (((1,), (1,)), ((), ())), preferred_element_type=jnp.float32
    )


def trans_times(left, right):
    return lax.dot_general(
        left, right, (((0,), (0,)), ((), ())), preferred_element_type=jnp.float32
    )


def low(value):
    return value.astype(jnp.bfloat16)


def high(value):
    return value.astype(jnp.float32)


class Groups:
    def __init__(self, fsdp, tp):
        self.fsdp, self.tp = fsdp, tp
        self.deep = fsdp // PLANE
        self.columns = [[b + PLANE * a for a in range(self.deep)] for b in range(PLANE)]

    def around(self, value, places):
        place = {b: i for i, b in enumerate(RING)}
        pairs = [
            (i, i - i % PLANE + RING[(place[i % PLANE] + places) % PLANE])
            for i in range(self.fsdp)
        ]
        return lax.ppermute(value, "fsdp", pairs)

    def along(self, value, places):
        pairs = [(i, (i + PLANE * places) % self.fsdp) for i in range(self.fsdp)]
        return lax.ppermute(value, "fsdp", pairs)

    def across(self, value, places):
        pairs = [(i, (i + places) % self.tp) for i in range(self.tp)]
        return lax.ppermute(value, "tp", pairs)

    def next_core(self, value):
        return lax.ppermute(value, "tp", [(i, i + 1) for i in range(self.tp - 1)])

    def last_core(self, value):
        return lax.ppermute(value, "tp", [(i + 1, i) for i in range(self.tp - 1)])

    def gather_plane(self, rows):
        half = rows.shape[0] // 2
        back = self.around(rows, 1)
        ahead = self.around(rows, -1)
        top = self.around(back[:half], 1)
        bottom = self.around(ahead[half:], -1)
        return jnp.concatenate([rows, back, top, bottom, ahead], 0)

    def reduce_plane(self, rows):
        count = rows.shape[0] // PLANE
        half = count // 2
        own, back, far, ahead = (rows[k * count : (k + 1) * count] for k in range(PLANE))
        top = self.around(low(far[:half]), -1)
        bottom = self.around(low(far[half:]), 1)
        back_sum = jnp.concatenate([low(high(back[:half]) + high(top)), low(back[half:])], 0)
        ahead_sum = jnp.concatenate([low(ahead[:half]), low(high(ahead[half:]) + high(bottom))], 0)
        one = self.around(back_sum, -1)
        two = self.around(ahead_sum, 1)
        return high(own) + high(one) + high(two)

    def gather_column(self, value):
        return lax.all_gather(
            value, "fsdp", axis=0, tiled=True, axis_index_groups=self.columns
        )

    def reduce_column(self, value):
        return lax.psum_scatter(
            value, "fsdp", scatter_dimension=0, tiled=True, axis_index_groups=self.columns
        )

    def cores(self, value):
        return [value] + [self.across(value, j) for j in range(1, self.tp)]

    def sum_cores(self, terms):
        total = terms[0]
        for j in range(1, self.tp):
            total = total + high(self.across(low(terms[j]), -j))
        return total

    def sum_all(self, value):
        total = value
        for j in range(1, self.tp):
            total = total + self.across(value, j)
        for move, size in ((self.around, PLANE), (self.along, self.deep)):
            part = total
            for j in range(1, size):
                total = total + move(part, j)
        return total

    def gather_features(self, value):
        me = lax.axis_index("fsdp")
        place = jnp.zeros((PLANE,), jnp.int32).at[jnp.array(RING)].set(jnp.arange(PLANE))
        mine = place[me % PLANE]
        flat = jnp.stack([value] + [self.around(value, j) for j in range(1, PLANE)])
        flat = flat[(mine - place) % PLANE]
        deep = jnp.stack([flat] + [self.along(flat, j) for j in range(1, self.deep)])
        deep = deep[(me // PLANE - jnp.arange(self.deep)) % self.deep]
        count, width = value.shape
        return deep.transpose(2, 0, 1, 3).reshape(count, self.fsdp * width)


def rms_scale(value):
    return lax.rsqrt(jnp.mean(value * value, -1, keepdims=True) + EPS)


def norm_back(value, scale, gain, grad_norm):
    scaled = grad_norm * gain
    grad_value = scale * scaled - value * scale**3 * jnp.mean(scaled * value, -1, keepdims=True)
    grad_gain = jnp.sum(grad_norm * value * scale, 0)
    return (grad_value, grad_gain)


def shift_down(value, places, before):
    return jnp.concatenate([before[:, 2 - places :], value[:, :-places]], 1)


def shift_up(value, places, after):
    return jnp.concatenate([value[:, places:], after[:, :places]], 1)


def on_device(
    tokens,
    seg_ids,
    norm1_gain,
    in_weight,
    conv_weight,
    out_weight,
    norm2_gain,
    gate_weight,
    up_weight,
    down_weight,
    cotangent,
    fsdp,
    tp,
):
    groups = Groups(fsdp, tp)
    deep = groups.deep
    micro_count, own_rows, width = tokens.shape
    rows = micro_count * own_rows
    share = in_weight.shape[2]
    hidden_share = gate_weight.shape[1]
    segments = PLANE * micro_count
    seq_len = seg_ids.shape[1]

    tokens_own = tokens.reshape(rows, width)
    cot_own = cotangent.reshape(rows, width)
    tokens_all = groups.gather_plane(tokens_own)

    gains = groups.gather_features(jnp.stack([norm1_gain, norm2_gain]))
    gain_one = high(gains[0])
    gain_two = high(gains[1])

    pad_rows = 16
    extra = jnp.zeros((pad_rows, width), jnp.bfloat16).at[0, : 3 * share].set(
        conv_weight.reshape(-1)
    )
    mixer = jnp.concatenate(
        [in_weight.transpose(1, 2, 0).reshape(3 * share, width), out_weight, extra], 0
    )
    mixer = groups.gather_column(mixer).reshape(deep, 4 * share + pad_rows, width)
    gate = groups.gather_column(gate_weight.T)
    up = groups.gather_column(up_weight.T)
    down = groups.gather_column(down_weight)

    taps = groups.cores(
        high(mixer[:, 4 * share, : 3 * share])
        .reshape(deep, 3, share)
        .transpose(1, 0, 2)
        .reshape(3, deep * share)
    )
    mats = groups.cores(
        mixer[:, : 4 * share]
        .reshape(deep, 4, share, width)
        .transpose(1, 0, 2, 3)
        .reshape(4, deep * share, width)
    )
    gate = groups.cores(gate)
    up = groups.cores(up)
    down = groups.cores(down)

    core = lax.axis_index("tp")
    same = []
    for places in (1, 2):
        equal = (seg_ids[:, places:] == seg_ids[:, :-places]).astype(jnp.float32)
        equal = jnp.concatenate([jnp.zeros((micro_count, places), jnp.float32), equal], 1)
        same.append(lax.dynamic_slice_in_dim(equal, core * own_rows, own_rows, 1))
    same = jnp.stack(same)
    same = jnp.stack([same] + [groups.around(same, k) for k in range(1, PLANE)])
    mask_one = same[:, 0].reshape(segments, own_rows, 1)
    mask_two = same[:, 1].reshape(segments, own_rows, 1)

    wide = high(tokens_all)
    scale_all = rms_scale(wide)
    normed = low(wide * scale_all * gain_one)
    parts = [
        [times_trans(normed, mat[k]).reshape(segments, own_rows, -1) for k in range(3)]
        for mat in mats
    ]
    gated_in = [part[1] * part[2] for part in parts]
    ends = [groups.next_core(value[:, -2:]) for value in gated_in]
    before = [ends[(j - 1) % tp] for j in range(tp)]
    one_back = [mask_one * shift_down(v, 1, b) for v, b in zip(gated_in, before)]
    two_back = [mask_two * shift_down(v, 2, b) for v, b in zip(gated_in, before)]
    conv_out = [
        tap[0] * v + tap[1] * one + tap[2] * two
        for tap, v, one, two in zip(taps, gated_in, one_back, two_back)
    ]
    mixed = [low(part[0] * out).reshape(PLANE * rows, -1) for part, out in zip(parts, conv_out)]
    mixer_out = sum(matmul(value, mat[3]) for value, mat in zip(mixed, mats))
    tokens_f = high(tokens_own)
    scale_one = rms_scale(tokens_f)
    resid = tokens_f + groups.reduce_plane(low(mixer_out))

    scale_two = rms_scale(resid)
    normed_two = groups.gather_plane(low(resid * scale_two * gain_two))
    cot_all = groups.gather_plane(cot_own)
    gate_pre = [times_trans(normed_two, mat) for mat in gate]
    up_pre = [times_trans(normed_two, mat) for mat in up]
    sigma = [jax.nn.sigmoid(value) for value in gate_pre]
    activated = [value * sig for value, sig in zip(gate_pre, sigma)]
    hidden = [low(act * value) for act, value in zip(activated, up_pre)]
    down_sum = groups.sum_cores([trans_times(value, cot_all) for value in hidden])
    down_grad = groups.reduce_column(low(down_sum))
    ffn_out = sum(matmul(value, mat) for value, mat in zip(hidden, down))

    grad_hidden = [times_trans(cot_all, mat) for mat in down]
    grad_gate = [
        low(gh * u * s * (1.0 + g * (1.0 - s)))
        for gh, u, s, g in zip(grad_hidden, up_pre, sigma, gate_pre)
    ]
    grad_up = [low(gh * act) for gh, act in zip(grad_hidden, activated)]
    back_two = sum(matmul(value, mat) for value, mat in zip(grad_gate, gate)) + sum(
        matmul(value, mat) for value, mat in zip(grad_up, up)
    )
    grad_normed_two = groups.reduce_plane(low(back_two))
    gate_sum = groups.sum_cores([trans_times(value, normed_two) for value in grad_gate])
    gate_grad = groups.reduce_column(low(gate_sum))
    up_sum = groups.sum_cores([trans_times(value, normed_two) for value in grad_up])
    up_grad = groups.reduce_column(low(up_sum))
    resid_back, norm_two_term = norm_back(resid, scale_two, gain_two, grad_normed_two)
    grad_resid = high(cot_own) + resid_back
    block_output = low(resid + groups.reduce_plane(low(ffn_out)))

    grad_mixer = groups.gather_plane(low(grad_resid))
    grad_mixed = [
        times_trans(grad_mixer, mat[3]).reshape(segments, own_rows, -1) for mat in mats
    ]
    grad_conv = [value * part[0] for value, part in zip(grad_mixed, parts)]
    masked_one = [mask_one * value for value in grad_conv]
    masked_two = [mask_two * value for value in grad_conv]
    starts = [
        groups.last_core(jnp.concatenate([one[:, :2], two[:, :2]], 0))
        for one, two in zip(masked_one, masked_two)
    ]
    after = [starts[(j + 1) % tp] for j in range(tp)]
    grad_gated = [
        tap[0] * value
        + tap[1] * shift_up(one, 1, edge[:segments])
        + tap[2] * shift_up(two, 2, edge[segments:])
        for tap, value, one, two, edge in zip(taps, grad_conv, masked_one, masked_two, after)
    ]
    grads = [
        [
            low(value).reshape(PLANE * rows, -1)
            for value in (gm * out, gg * part[2], gg * part[1])
        ]
        for gm, out, gg, part in zip(grad_mixed, conv_out, grad_gated, parts)
    ]
    back_one = sum(
        sum(matmul(value, mat[k]) for k, value in enumerate(grad)) for grad, mat in zip(grads, mats)
    )
    grad_normed = groups.reduce_plane(low(back_one))

    def column_sum(terms):
        return groups.reduce_column(low(groups.sum_cores(terms)))

    out_grad = column_sum([trans_times(value, grad_mixer) for value in mixed])
    in_grad = [
        column_sum([trans_times(grad[k], normed) for grad in grads]) for k in range(3)
    ]
    conv_term = groups.sum_cores(
        [
            jnp.stack([jnp.sum(gc * value, (0, 1)) for value in (gi, one, two)])
            for gc, gi, one, two in zip(grad_conv, gated_in, one_back, two_back)
        ]
    )
    conv_sum = conv_term
    for k in range(1, deep):
        conv_sum = conv_sum + groups.along(conv_term, k)
    chip = lax.axis_index("fsdp")
    conv_grad = lax.dynamic_slice_in_dim(
        conv_sum.reshape(3, deep * share), chip // PLANE * share, share, 1
    )
    input_back, norm_one_term = norm_back(tokens_f, scale_one, gain_one, grad_normed)
    input_grad = low(grad_resid + input_back)
    gain_sums = groups.sum_all(jnp.stack([norm_one_term, norm_two_term]))
    gain_share = norm1_gain.shape[0]
    gain_grads = lax.dynamic_slice_in_dim(gain_sums, chip * gain_share, gain_share, 1)
    return (
        block_output.reshape(tokens.shape),
        input_grad.reshape(tokens.shape),
        gain_grads[0],
        high(jnp.stack(in_grad)).transpose(2, 0, 1),
        conv_grad,
        high(out_grad),
        gain_grads[1],
        high(gate_grad).T,
        high(up_grad).T,
        high(down_grad),
    )


def solution(mesh):
    fsdp, tp = mesh.shape["fsdp"], mesh.shape["tp"]

    def body(*args):
        return on_device(*args, fsdp, tp)

    return jax.shard_map(
        body,
        mesh=mesh,
        in_specs=(
            P(None, ("fsdp", "tp"), None),
            P(None, "fsdp"),
            P("fsdp"),
            P(None, None, ("fsdp", "tp")),
            P(None, ("fsdp", "tp")),
            P(("fsdp", "tp"), None),
            P("fsdp"),
            P(None, ("fsdp", "tp")),
            P(None, ("fsdp", "tp")),
            P(("fsdp", "tp"), None),
            P(None, ("fsdp", "tp"), None),
        ),
        out_specs=(
            P(None, ("fsdp", "tp"), None),
            P(None, ("fsdp", "tp"), None),
            P("fsdp"),
            P(None, None, ("fsdp", "tp")),
            P(None, ("fsdp", "tp")),
            P(("fsdp", "tp"), None),
            P("fsdp"),
            P(None, ("fsdp", "tp")),
            P(None, ("fsdp", "tp")),
            P(("fsdp", "tp"), None),
        ),
        check_vma=False,
    )
```

```python
import jax
import jax.numpy as jnp
from jax import lax
from jax.experimental import pallas as pl
from jax.experimental.pallas import tpu as pltpu
from jax.sharding import PartitionSpec as P

EPS = 1e-05


def matmul(left, right):
    return jnp.dot(left, right, preferred_element_type=jnp.float32)


def times_trans(left, right):
    return lax.dot_general(
        left, right, (((1,), (1,)), ((), ())), preferred_element_type=jnp.float32
    )


def trans_times(left, right):
    return lax.dot_general(
        left, right, (((0,), (0,)), ((), ())), preferred_element_type=jnp.float32
    )


def low(value):
    return value.astype(jnp.bfloat16)


def high(value):
    return value.astype(jnp.float32)


def kernel_call(body, grid, in_specs, out_specs, out_shape, flops, moved):
    return pl.pallas_call(
        body,
        grid=grid,
        in_specs=in_specs,
        out_specs=out_specs,
        out_shape=out_shape,
        compiler_params=pltpu.CompilerParams(
            dimension_semantics=("arbitrary",), vmem_limit_bytes=48 * 1024 * 1024
        ),
        cost_estimate=pl.CostEstimate(flops=1, bytes_accessed=1, transcendentals=0),
    )


def size_of(*arrays):
    return sum(array.size * array.dtype.itemsize for array in arrays)


def whole(shape):
    return pl.BlockSpec(shape, lambda i: (0, 0), pipeline_mode=pl.Buffered(1))


def sum_of_products(lefts, rights, tile=512):
    rows, width = lefts[0].shape[0], rights[0].shape[1]
    count = len(lefts)

    def body(*refs):
        total = matmul(refs[0][...], refs[count][...])
        for k in range(1, count):
            total = total + matmul(refs[k][...], refs[count + k][...])
        refs[-1][...] = low(total)

    depth = sum(left.shape[1] for left in lefts)
    return kernel_call(
        body,
        (width // tile,),
        [whole(left.shape) for left in lefts]
        + [pl.BlockSpec((right.shape[0], tile), lambda i: (0, i)) for right in rights],
        pl.BlockSpec((rows, tile), lambda i: (0, i)),
        jax.ShapeDtypeStruct((rows, width), jnp.bfloat16),
        2 * rows * depth * width,
        size_of(*lefts, *rights) + 2 * rows * width,
    )(*lefts, *rights)


def ffn_ahead(normed, gate, up, tile=256):
    rows, width = normed.shape
    units = gate.shape[0]
    tile = min(tile, rows)

    def body(normed_ref, gate_ref, up_ref, hidden_ref, gate_slope_ref, up_slope_ref):
        pre = times_trans(normed_ref[...], gate_ref[...])
        value = times_trans(normed_ref[...], up_ref[...])
        sigma = jax.nn.sigmoid(pre)
        activated = pre * sigma
        hidden_ref[...] = low(activated * value)
        gate_slope_ref[...] = low(value * sigma * (1.0 + pre * (1.0 - sigma)))
        up_slope_ref[...] = low(activated)

    out = jax.ShapeDtypeStruct((rows, units), jnp.bfloat16)
    spec = pl.BlockSpec((tile, units), lambda i: (i, 0))
    return kernel_call(
        body,
        (rows // tile,),
        [pl.BlockSpec((tile, width), lambda i: (i, 0)), whole(gate.shape), whole(up.shape)],
        [spec] * 3,
        [out] * 3,
        4 * rows * width * units,
        size_of(normed, gate, up) + 6 * rows * units,
    )(normed, gate, up)


def ffn_back(grad, down, gate, up, gate_slope, up_slope, tile=256):
    rows, width = grad.shape
    units = down[0].shape[0]
    tile = min(tile, rows)
    count = len(down)
    mats = [mat for group in zip(down, gate, up) for mat in group]
    slopes = [slope for group in zip(gate_slope, up_slope) for slope in group]

    wide = -(-units // 256) * 256

    def body(grad_ref, *refs):
        mat_refs, slope_refs = refs[: 3 * count], refs[3 * count : 5 * count]
        out_refs, total_ref = refs[5 * count : 7 * count], refs[7 * count]
        downs, others, pieces, sems = refs[7 * count + 1 :]
        first = pl.program_id(0) == 0
        copies = []
        for j in range(count):
            targets = [downs.at[j]]
            targets += [others.at[pl.ds((2 * j + k) * wide, units)] for k in range(2)]
            for k, target in enumerate(targets):
                at = 3 * j + k
                copies.append(pltpu.make_async_copy(mat_refs[at], target, sems.at[at]))

        @pl.when(first)
        def _():
            for copy in copies[::3] + copies[1::3] + copies[2::3]:
                copy.start()
            if wide > units:
                pieces[...] = jnp.zeros_like(pieces)
                for at in range(2 * count):
                    others[at * wide + units : (at + 1) * wide, :] = jnp.zeros(
                        (wide - units, width), jnp.bfloat16
                    )
            for copy in copies[::3]:
                copy.wait()

        for j in range(count):
            grad_hidden = times_trans(grad_ref[...], downs[j])
            for k in range(2):
                at = 2 * j + k
                piece = low(grad_hidden * high(slope_refs[at][...]))
                out_refs[at][...] = piece
                pieces[:, at * wide : at * wide + units] = piece

        @pl.when(first)
        def _():
            for copy in copies[1::3] + copies[2::3]:
                copy.wait()

        total_ref[...] = low(matmul(pieces[...], others[...]))

    out = jax.ShapeDtypeStruct((rows, units), jnp.bfloat16)
    spec = pl.BlockSpec((tile, units), lambda i: (i, 0))
    row_spec = pl.BlockSpec((tile, width), lambda i: (i, 0))
    found = pl.pallas_call(
        body,
        grid=(rows // tile,),
        in_specs=[row_spec]
        + [pl.BlockSpec(memory_space=pl.ANY)] * (3 * count)
        + [spec] * (2 * count),
        out_specs=[spec] * (2 * count) + [row_spec],
        out_shape=[out] * (2 * count) + [jax.ShapeDtypeStruct((rows, width), jnp.bfloat16)],
        scratch_shapes=[
            pltpu.VMEM((count, units, width), jnp.bfloat16),
            pltpu.VMEM((2 * count * wide, width), jnp.bfloat16),
            pltpu.VMEM((tile, 2 * count * wide), jnp.bfloat16),
            pltpu.SemaphoreType.DMA((3 * count,)),
        ],
        compiler_params=pltpu.CompilerParams(
            dimension_semantics=("arbitrary",), vmem_limit_bytes=48 * 1024 * 1024
        ),
        cost_estimate=pl.CostEstimate(flops=1, bytes_accessed=1, transcendentals=0),
    )(grad, *mats, *slopes)
    return [found[2 * j] for j in range(count)], [found[2 * j + 1] for j in range(count)], found[-1]


class Order:
    def __init__(self):
        self.last = ()

    def __call__(self, *values):
        values = lax.optimization_barrier((values, self.last))[0]
        return values if len(values) > 1 else values[0]

    def did(self, *results):
        self.last = results

    def wait(self, *results):
        self.last = (*self.last, *results)


class Groups:
    def __init__(self, fsdp, tp, order):
        self.fsdp, self.tp, self.order = fsdp, tp, order
        self.deep = fsdp // 4
        self.columns = [[b + 4 * a for a in range(self.deep)] for b in range(4)]

    def along(self, value):
        pairs = [(i, (i + 4) % self.fsdp) for i in range(self.fsdp)]
        return lax.ppermute(value, "fsdp", pairs)

    def swap(self, value, bit):
        return lax.ppermute(value, "fsdp", [(i, i ^ bit) for i in range(self.fsdp)])

    def across(self, value, places):
        pairs = [(i, (i + places) % self.tp) for i in range(self.tp)]
        return lax.ppermute(value, "tp", pairs)

    def next_core(self, value):
        return lax.ppermute(value, "tp", [(i, i + 1) for i in range(self.tp - 1)])

    def last_core(self, value):
        return lax.ppermute(value, "tp", [(i + 1, i) for i in range(self.tp - 1)])

    def cores(self, value):
        value = self.order(value)
        return [value] + [self.across(value, j) for j in range(1, self.tp)]

    def sum_cores(self, sent):
        return [self.across(self.order(value), -j) for j, value in enumerate(sent, 1)]

    def sum_cores_of(self, value):
        total = value
        for j in range(1, self.tp):
            total = total + self.across(value, j)
        return total

    def sum_bits(self, value, bits):
        for bit in bits:
            value = value + self.swap(value, bit)
        return value

    def gather_ordered(self, value):
        return lax.all_gather(
            value, "fsdp", axis=0, tiled=True, axis_index_groups=self.columns
        )

    def reduce_ordered(self, value):
        return lax.psum_scatter(
            value, "fsdp", scatter_dimension=0, tiled=True, axis_index_groups=self.columns
        )

    def stack(self, value, bits):
        stack = value[None]
        for bit in bits:
            stack = jnp.concatenate([stack, self.swap(self.order(stack), bit)], 0)
        return stack


class Rows:
    def __init__(self, groups, rows):
        self.groups, self.rows = groups, groups.order(rows)
        self.one = groups.swap(self.rows, 1)
        self.two = groups.swap(self.rows, 2)

    def middle(self):
        half = self.rows.shape[0] // 2
        self.groups.order.wait(self.one, self.two)
        top, bottom = self.groups.order(self.two[:half], self.one[half:])
        self.top = self.groups.swap(top, 1)
        self.bottom = self.groups.swap(bottom, 2)

    def end(self):
        order = self.groups.order
        order.wait(self.top, self.bottom)
        return jnp.concatenate(
            order(self.rows, self.one, self.two, self.top, self.bottom), 0
        )


class Sums:
    def __init__(self, groups, blocks, late=False):
        self.groups, self.late, blocks = groups, late, groups.order(blocks)
        own, one, two, far = (
            (block[: block.shape[0] // 2], block[block.shape[0] // 2 :])
            for block in jnp.split(blocks, 4)
        )
        self.own, self.one, self.two = own, one, two
        self.far = groups.swap(far[0], 1), groups.swap(far[1], 2)
        if not late:
            self.direct = groups.swap(one[0], 1), groups.swap(two[1], 2)

    def middle(self):
        order, swap = self.groups.order, self.groups.swap
        order.wait(self.far)
        first, second = order(*self.far)
        second = low(high(self.one[1]) + high(second))
        first = low(high(self.two[0]) + high(first))
        if self.late:
            second = jnp.concatenate([self.one[0], second], 0)
            first = jnp.concatenate([first, self.two[1]], 0)
        order.did(first, second)
        first, second = order(first, second)
        self.summed = swap(second, 1), swap(first, 2)

    def end(self):
        order = self.groups.order
        if self.late:
            order.wait(self.summed)
            one, two = order(*self.summed)
            return high(jnp.concatenate(self.own, 0)) + high(one) + high(two)
        order.wait(self.direct, self.summed)
        (one_first, two_second), (one_second, two_first) = order(self.direct, self.summed)
        return jnp.concatenate(
            [
                high(self.own[0]) + high(one_first) + high(two_first),
                high(self.own[1]) + high(one_second) + high(two_second),
            ],
            0,
        )


def after(value, *before):
    return lax.optimization_barrier((value, *before))[0]


def rms_scale(value):
    return lax.rsqrt(jnp.mean(value * value, -1, keepdims=True) + EPS)


def norm_back(value, scale, gain, grad_norm):
    scaled = grad_norm * gain
    return scale * scaled - value * scale**3 * jnp.mean(scaled * value, -1, keepdims=True)


def shift_down(value, places, before):
    return jnp.concatenate([before[:, 2 - places :], value[:, :-places]], 1)


def shift_up(value, places, after):
    return jnp.concatenate([value[:, places:], after[:, :places]], 1)


def on_device(
    tokens,
    seg_ids,
    norm1_gain,
    in_weight,
    conv_weight,
    out_weight,
    norm2_gain,
    gate_weight,
    up_weight,
    down_weight,
    cotangent,
    fsdp,
    tp,
):
    order = Order()
    groups = Groups(fsdp, tp, order)
    deep = groups.deep
    micro_count, own_rows, width = tokens.shape
    rows = micro_count * own_rows
    share = in_weight.shape[2]
    hidden_share = gate_weight.shape[1]
    wide_share = deep * share
    segments = 4 * micro_count
    chip = lax.axis_index("fsdp")
    core = lax.axis_index("tp")

    plane_bits, column_bits, bit = (1, 2), [], 4
    while bit < fsdp:
        column_bits.append(bit)
        bit *= 2

    mixer_own = jnp.concatenate(
        [in_weight.transpose(1, 2, 0).reshape(3 * share, width), out_weight], 0
    )
    mixer_all = groups.gather_ordered(mixer_own)
    gate_own, up_own = gate_weight.T, up_weight.T
    gate_all = groups.gather_ordered(after(gate_own, mixer_own))
    up_all = groups.gather_ordered(after(up_own, gate_own))
    down_all = groups.gather_ordered(after(down_weight, up_own))

    plane = chip // 4
    same = []
    for places in (1, 2):
        equal = (seg_ids[:, places:] == seg_ids[:, :-places]).astype(jnp.float32)
        equal = jnp.concatenate([jnp.zeros((micro_count, places), jnp.float32), equal], 1)
        same.append(lax.dynamic_slice_in_dim(equal, core * own_rows, own_rows, 1))
    tokens_own = tokens.reshape(rows, width)
    cot_own = cotangent.reshape(rows, width)
    token_rows = Rows(groups, tokens_own)
    gains = groups.stack(jnp.stack([norm1_gain, norm2_gain]), column_bits)
    order.wait(gains, gate_own, up_own)
    taps = groups.stack(conv_weight, column_bits)
    order.wait(taps)
    gains = groups.stack(gains, plane_bits[:1])
    same = groups.stack(jnp.stack(same), plane_bits[:1])
    token_rows.middle()
    order.wait(gains, same)
    gains = groups.stack(gains, plane_bits[1:])
    same = groups.stack(same, plane_bits[1:])
    order.wait(gains, same)
    tokens_all = token_rows.end()
    order.did(tokens_all)
    taps = taps[jnp.arange(deep) ^ plane].transpose(1, 0, 2).reshape(3, wide_share)
    taps = [high(tap) for tap in groups.cores(taps)]
    order.wait(taps)
    cot_rows = Rows(groups, cot_own)
    same = same.reshape(4, 2, micro_count, own_rows)
    mask_one = same[:, 0].reshape(segments, own_rows, 1)
    mask_two = same[:, 1].reshape(segments, own_rows, 1)
    gains = gains.reshape(4, deep, 2, -1).swapaxes(0, 1).reshape(fsdp, 2, -1)
    gains = gains[jnp.arange(fsdp) ^ chip].transpose(1, 0, 2).reshape(2, width)
    gain_one = high(gains[0])
    gain_two = high(gains[1])
    tokens_now, gain_now = order(tokens_all, gain_one)
    wide = high(tokens_now)
    scale_all = rms_scale(wide)
    normed = low(wide * scale_all * gain_now)
    order.did(normed)
    cot_rows.middle()
    order.wait(mixer_all)

    mixers = groups.cores(mixer_all)
    in_mats, out_mats, parts, gated_in = [], [], [], []
    for j in range(tp):
        if j:
            order.wait(mixers[j])
        mat = order(mixers[j]).reshape(deep, 4, share, width).transpose(1, 0, 2, 3)
        in_mats.append(mat[:3].reshape(3 * wide_share, width))
        out_mats.append(mat[3].reshape(wide_share, width))
        order.did(in_mats[-1], out_mats[-1])
        normed_now, mat = order(normed, in_mats[-1])
        projected = times_trans(normed_now, mat).reshape(segments, own_rows, 3 * wide_share)
        parts.append([projected[..., k * wide_share : (k + 1) * wide_share] for k in range(3)])
        gated_in.append(parts[-1][1] * parts[-1][2])
        order.did(parts[-1], gated_in[-1])
    ends = groups.next_core(order(jnp.stack([value[:, -2:] for value in gated_in])))
    order.wait(ends)
    parts, gated_in, ends = order(parts, gated_in, ends)
    before = [ends[(j - 1) % tp] for j in range(tp)]
    one_back = [mask_one * shift_down(v, 1, b) for v, b in zip(gated_in, before)]
    two_back = [mask_two * shift_down(v, 2, b) for v, b in zip(gated_in, before)]
    conv_out = [
        tap[0] * v + tap[1] * one + tap[2] * two
        for tap, v, one, two in zip(taps, gated_in, one_back, two_back)
    ]
    mixed = [low(part[0] * out).reshape(4 * rows, -1) for part, out in zip(parts, conv_out)]
    mixer_out = sum_of_products(mixed, out_mats)
    order.did(mixer_out)
    cot_all = cot_rows.end()
    order.wait(cot_all)
    mixer_sums = Sums(groups, mixer_out)
    mixer_sums.middle()
    mixer_sum = mixer_sums.end()
    order.wait(gate_all)
    mixer_sum, tokens_now = order(mixer_sum, tokens_own)
    tokens_f = high(tokens_own)
    resid = high(tokens_now) + mixer_sum

    scale_two = rms_scale(resid)
    normed_own = low(resid * scale_two * gain_two)
    order.did(normed_own)
    two_rows = Rows(groups, normed_own)
    two_rows.middle()
    gate = groups.cores(gate_all)
    order.wait(gate)
    order.wait(up_all)
    up = groups.cores(up_all)
    normed_two = two_rows.end()
    order.did(normed_two)
    hidden, gate_slope, up_slope = [], [], []
    for j in range(tp):
        if j:
            order.wait(up[j])
        found = ffn_ahead(*order(normed_two, gate[j], up[j]))
        order.did(*found)
        for kept, value in zip((hidden, gate_slope, up_slope), found):
            kept.append(value)
    def core_terms(left, right):
        left, right = order(left, right)
        sent = [low(trans_times(value, right)) for value in left[1:]]
        order.did(sent)
        return groups.sum_cores(sent)

    def own_term(left, right, got):
        order.wait(got)
        left, right, got = order(left, right, got)
        total = trans_times(left, right)
        for value in got:
            total = total + high(value)
        total = low(total)
        order.did(total)
        return total

    got = core_terms(hidden, cot_all)
    down_total = own_term(hidden[0], cot_all, got)
    order.wait(down_all)
    down_grad = groups.reduce_ordered(order(down_total))
    down_mats = groups.cores(down_all)
    order.wait(down_mats)
    grad_gate, grad_up, back_two = ffn_back(
        *order(cot_all, down_mats, gate, up, gate_slope, up_slope)
    )
    order.did(grad_gate, grad_up, back_two)
    two_sums = Sums(groups, back_two)
    gate_got = core_terms(grad_gate, normed_two)
    gate_total = own_term(grad_gate[0], normed_two, gate_got)
    two_sums.middle()
    order.wait(down_grad)
    gate_grad = groups.reduce_ordered(order(gate_total))
    up_got = core_terms(grad_up, normed_two)
    grad_normed_two = two_sums.end()
    resid_back = norm_back(resid, scale_two, gain_two, grad_normed_two)
    grad_resid = high(cot_own) + resid_back
    grad_low = low(grad_resid)
    order.did(grad_low)
    mixer_rows = Rows(groups, grad_low)
    up_total = own_term(grad_up[0], normed_two, up_got)
    mixer_rows.middle()
    norm_two_term = jnp.sum(grad_normed_two * resid * scale_two, 0)
    order.wait(gate_grad)
    up_grad = groups.reduce_ordered(order(up_total))
    hidden_now, down_now = order(hidden, down_mats)
    ffn_out = sum_of_products(hidden_now, down_now)
    order.did(ffn_out, norm_two_term)
    ffn_sums = Sums(groups, ffn_out, True)
    grad_mixer = mixer_rows.end()
    order.did(grad_mixer)

    grad_now, mats_now = order(grad_mixer, out_mats)
    grad_mixed = [
        times_trans(grad_now, mat).reshape(segments, own_rows, -1) for mat in mats_now
    ]
    grad_conv = [value * part[0] for value, part in zip(grad_mixed, parts)]
    grad_b = [
        low(value * out).reshape(4 * rows, -1) for value, out in zip(grad_mixed, conv_out)
    ]
    masked_one = [mask_one * value for value in grad_conv]
    masked_two = [mask_two * value for value in grad_conv]
    edges = jnp.stack(
        [jnp.concatenate([one[:, :2], two[:, :2]], 0) for one, two in zip(masked_one, masked_two)]
    )
    order.did(grad_b, grad_conv, edges)
    starts = groups.last_core(order(edges))
    ffn_sums.middle()
    b_got = core_terms(grad_b, normed)
    out_got = core_terms(mixed, grad_mixer)
    order.wait(starts)
    grad_conv_now, masked_one, masked_two, starts = order(
        grad_conv, masked_one, masked_two, starts
    )
    after_edge = [starts[(j + 1) % tp] for j in range(tp)]
    grad_gated = [
        tap[0] * value
        + tap[1] * shift_up(one, 1, edge[:segments])
        + tap[2] * shift_up(two, 2, edge[segments:])
        for tap, value, one, two, edge in zip(
            taps, grad_conv_now, masked_one, masked_two, after_edge
        )
    ]
    grad_cx = [
        jnp.concatenate([low(gg * part[k]).reshape(4 * rows, -1) for k in (2, 1)], 1)
        for gg, part in zip(grad_gated, parts)
    ]
    order.did(grad_cx)
    cx_got = core_terms(grad_cx, normed)
    b_total = own_term(grad_b[0], normed, b_got)
    out_total = own_term(mixed[0], grad_mixer, out_got)
    cx_total = own_term(grad_cx[0], normed, cx_got)
    mixer_total = (
        jnp.concatenate([b_total, cx_total, out_total], 0)
        .reshape(4, deep, share, width)
        .transpose(1, 0, 2, 3)
        .reshape(4 * wide_share, width)
    )
    order.did(mixer_total)
    order.wait(up_grad)
    block_output = low(resid + ffn_sums.end())
    order.did(block_output)
    mixer_grad = groups.reduce_ordered(order(mixer_total))
    b_mats = [mat[:wide_share] for mat in in_mats]
    cx_mats = [mat[wide_share:] for mat in in_mats]
    back_one = sum_of_products(*order(grad_b + grad_cx, b_mats + cx_mats))
    order.did(back_one)
    one_rows = Sums(groups, back_one)
    back_now = order(back_one)
    norm_one_term = jnp.sum(high(back_now) * wide * scale_all, 0)
    conv_terms = [
        jnp.stack([jnp.sum(gc * value, (0, 1)) for value in (gi, one, two)])
        for gc, gi, one, two in zip(grad_conv, gated_in, one_back, two_back)
    ]
    order.did(norm_one_term, conv_terms)
    one_rows.middle()
    conv_sum = conv_terms[0]
    for j in range(1, tp):
        conv_sum = conv_sum + groups.across(order(conv_terms[j]), -j)
    gain_sums = groups.sum_cores_of(order(jnp.stack([norm_one_term, norm_two_term])))
    conv_sum = groups.sum_bits(conv_sum, column_bits)
    gain_sums = groups.sum_bits(gain_sums, column_bits)
    conv_total = lax.dynamic_slice_in_dim(conv_sum, plane * share, share, 1)
    order.wait(conv_total, gain_sums)
    grad_normed = one_rows.end()
    input_back = norm_back(tokens_f, rms_scale(tokens_f), gain_one, grad_normed)
    input_grad = low(grad_resid + input_back)
    order.did(input_grad)
    gain_sums = groups.sum_bits(order(gain_sums), plane_bits)
    gate_grad, up_grad = order(gate_grad, up_grad)
    gate_grad, up_grad = high(gate_grad).T, high(up_grad).T
    order.did(gate_grad, up_grad)
    order.wait(mixer_grad)
    mixer_grad = high(mixer_grad).reshape(4, share, width)
    gain_share = norm1_gain.shape[0]
    gain_grads = lax.dynamic_slice_in_dim(gain_sums, chip * gain_share, gain_share, 1)
    return (
        block_output.reshape(tokens.shape),
        input_grad.reshape(tokens.shape),
        gain_grads[0],
        mixer_grad[:3].transpose(2, 0, 1),
        conv_total,
        mixer_grad[3],
        gain_grads[1],
        gate_grad,
        up_grad,
        high(down_grad),
    )


def solution(mesh):
    fsdp, tp = mesh.shape["fsdp"], mesh.shape["tp"]

    def body(*args):
        return on_device(*args, fsdp, tp)

    return jax.shard_map(
        body,
        mesh=mesh,
        in_specs=(
            P(None, ("fsdp", "tp"), None),
            P(None, "fsdp"),
            P("fsdp"),
            P(None, None, ("fsdp", "tp")),
            P(None, ("fsdp", "tp")),
            P(("fsdp", "tp"), None),
            P("fsdp"),
            P(None, ("fsdp", "tp")),
            P(None, ("fsdp", "tp")),
            P(("fsdp", "tp"), None),
            P(None, ("fsdp", "tp"), None),
        ),
        out_specs=(
            P(None, ("fsdp", "tp"), None),
            P(None, ("fsdp", "tp"), None),
            P("fsdp"),
            P(None, None, ("fsdp", "tp")),
            P(None, ("fsdp", "tp")),
            P(("fsdp", "tp"), None),
            P("fsdp"),
            P(None, ("fsdp", "tp")),
            P(None, ("fsdp", "tp")),
            P(("fsdp", "tp"), None),
        ),
        check_vma=False,
    )
```

```python
import jax
import jax.numpy as jnp
from jax import lax
from jax.experimental import pallas as pl
from jax.experimental.pallas import tpu as pltpu
from jax.sharding import PartitionSpec as P

EPS = 1e-05


def matmul(left, right):
    return jnp.dot(left, right, preferred_element_type=jnp.float32)


def times_trans(left, right):
    return lax.dot_general(
        left, right, (((1,), (1,)), ((), ())), preferred_element_type=jnp.float32
    )


def trans_times(left, right):
    return lax.dot_general(
        left, right, (((0,), (0,)), ((), ())), preferred_element_type=jnp.float32
    )


def low(value):
    return value.astype(jnp.bfloat16)


def high(value):
    return value.astype(jnp.float32)


def whole(shape):
    return pl.BlockSpec(shape, lambda i: (0, 0), pipeline_mode=pl.Buffered(1))


def sum_of_products(lefts, rights, tile=256):
    rows, width = lefts[0].shape[0], rights[0].shape[1]
    count = len(lefts)
    tile = min(tile, rows)
    depths = [left.shape[1] for left in lefts]
    starts, depth = [], 0
    for size in depths:
        starts.append(depth)
        depth += -(-size // 256) * 256
    limit = 2 * depth * (width + 3 * tile) + 8 * tile * width + 4 * 1024 * 1024

    def body(*refs):
        left_refs, right_refs, out_ref = refs[:count], refs[count : 2 * count], refs[2 * count]
        side, stacked, sems = refs[2 * count + 1 :]
        copies = [
            pltpu.make_async_copy(right, stacked.at[pl.ds(start, size)], sems.at[k])
            for k, (right, start, size) in enumerate(zip(right_refs, starts, depths))
        ]

        @pl.when(pl.program_id(0) == 0)
        def _():
            for copy in copies:
                copy.start()
            for start, end, size in zip(starts, starts[1:] + [depth], depths):
                if start + size < end:
                    side[:, start + size : end] = jnp.zeros(
                        (tile, end - start - size), jnp.bfloat16
                    )
                    stacked[start + size : end, :] = jnp.zeros(
                        (end - start - size, width), jnp.bfloat16
                    )
            for copy in copies:
                copy.wait()

        for left, start, size in zip(left_refs, starts, depths):
            side[:, start : start + size] = left[...]
        out_ref[...] = low(matmul(side[...], stacked[...]))

    return pl.pallas_call(
        body,
        grid=(rows // tile,),
        in_specs=[pl.BlockSpec((tile, size), lambda i: (i, 0)) for size in depths]
        + [pl.BlockSpec(memory_space=pl.ANY)] * count,
        out_specs=pl.BlockSpec((tile, width), lambda i: (i, 0)),
        out_shape=jax.ShapeDtypeStruct((rows, width), jnp.bfloat16),
        scratch_shapes=[
            pltpu.VMEM((tile, depth), jnp.bfloat16),
            pltpu.VMEM((depth, width), jnp.bfloat16),
            pltpu.SemaphoreType.DMA((count,)),
        ],
        compiler_params=pltpu.CompilerParams(
            dimension_semantics=("arbitrary",), vmem_limit_bytes=limit
        ),
        cost_estimate=pl.CostEstimate(flops=1, bytes_accessed=1, transcendentals=0),
    )(*lefts, *rights)


def rows_product(left, right, tile=256):
    rows, width = left.shape
    count = right.shape[0]
    tile = min(tile, rows)

    def body(left_ref, right_ref, out_ref):
        out_ref[...] = low(times_trans(left_ref[...], right_ref[...]))

    return pl.pallas_call(
        body,
        grid=(rows // tile,),
        in_specs=[pl.BlockSpec((tile, width), lambda i: (i, 0)), whole(right.shape)],
        out_specs=pl.BlockSpec((tile, count), lambda i: (i, 0)),
        out_shape=jax.ShapeDtypeStruct((rows, count), jnp.bfloat16),
        compiler_params=pltpu.CompilerParams(
            dimension_semantics=("arbitrary",), vmem_limit_bytes=12 * 1024 * 1024
        ),
        cost_estimate=pl.CostEstimate(flops=1, bytes_accessed=1, transcendentals=0),
    )(left, right)


def columns_product(left, right, more=(), flops=1, far=False, tile=512):
    rows, count = left.shape
    width = right.shape[1]

    def body(left_ref, right_ref, *refs):
        total = trans_times(left_ref[...], right_ref[...])
        for ref in refs[:-1]:
            total = total + high(ref[...])
        refs[-1][...] = low(total)

    spec = pl.BlockSpec((count, tile), lambda i: (0, i))
    return pl.pallas_call(
        body,
        grid=(width // tile,),
        in_specs=[whole(left.shape), pl.BlockSpec((rows, tile), lambda i: (0, i))]
        + [spec] * len(more),
        out_specs=spec,
        out_shape=(pltpu.HBM if far else jax.ShapeDtypeStruct)((count, width), jnp.bfloat16),
        compiler_params=pltpu.CompilerParams(
            dimension_semantics=("arbitrary",), vmem_limit_bytes=14 * 1024 * 1024
        ),
        cost_estimate=pl.CostEstimate(flops=flops, bytes_accessed=1, transcendentals=0),
    )(left, right, *more)


def ffn_call(body, lefts, rights, slopes, count, tile=256):
    rows, units = lefts[0].shape[0], rights[0].shape[0]
    tile = min(tile, rows)
    spec = pl.BlockSpec((tile, units), lambda i: (i, 0))
    return pl.pallas_call(
        body,
        grid=(rows // tile,),
        in_specs=[pl.BlockSpec((tile, left.shape[1]), lambda i: (i, 0)) for left in lefts]
        + [whole(right.shape) for right in rights]
        + [spec] * len(slopes),
        out_specs=[spec] * count,
        out_shape=[jax.ShapeDtypeStruct((rows, units), jnp.bfloat16)] * count,
        compiler_params=pltpu.CompilerParams(
            dimension_semantics=("arbitrary",), vmem_limit_bytes=20 * 1024 * 1024
        ),
        cost_estimate=pl.CostEstimate(flops=1, bytes_accessed=1, transcendentals=0),
    )(*lefts, *rights, *slopes)


def ffn_ahead(normed, gate, up):
    def body(normed_ref, gate_ref, up_ref, hidden_ref, gate_slope_ref, up_slope_ref):
        pre = times_trans(normed_ref[...], gate_ref[...])
        value = times_trans(normed_ref[...], up_ref[...])
        sigma = jax.nn.sigmoid(pre)
        activated = pre * sigma
        hidden_ref[...] = low(activated * value)
        gate_slope_ref[...] = low(value * sigma * (1.0 + pre * (1.0 - sigma)))
        up_slope_ref[...] = low(activated)

    return ffn_call(body, [normed], [gate, up], [], 3)


def ffn_back(grad, down, gate_slope, up_slope):
    def body(grad_ref, down_ref, gate_slope_ref, up_slope_ref, gate_ref, up_ref):
        grad_hidden = times_trans(grad_ref[...], down_ref[...])
        gate_ref[...] = low(grad_hidden * high(gate_slope_ref[...]))
        up_ref[...] = low(grad_hidden * high(up_slope_ref[...]))

    return ffn_call(body, [grad], [down], [gate_slope, up_slope], 2)


class Order:
    def __init__(self):
        self.last = ()

    def __call__(self, *values):
        values = lax.optimization_barrier((values, self.last))[0]
        return values if len(values) > 1 else values[0]

    def did(self, *results):
        self.last = results

    def wait(self, *results):
        self.last = (*self.last, *results)


class Groups:
    def __init__(self, fsdp, tp, order):
        self.fsdp, self.tp, self.order = fsdp, tp, order
        self.deep = fsdp // 4
        self.columns = [[b + 4 * a for a in range(self.deep)] for b in range(4)]

    def along(self, value):
        pairs = [(i, (i + 4) % self.fsdp) for i in range(self.fsdp)]
        return lax.ppermute(value, "fsdp", pairs)

    def swap(self, value, bit):
        return lax.ppermute(value, "fsdp", [(i, i ^ bit) for i in range(self.fsdp)])

    def across(self, value, places):
        pairs = [(i, (i + places) % self.tp) for i in range(self.tp)]
        return lax.ppermute(value, "tp", pairs)

    def next_core(self, value):
        return lax.ppermute(value, "tp", [(i, i + 1) for i in range(self.tp - 1)])

    def last_core(self, value):
        return lax.ppermute(value, "tp", [(i + 1, i) for i in range(self.tp - 1)])

    def cores(self, value):
        value = self.order(value)
        return [value] + [self.across(value, j) for j in range(1, self.tp)]

    def sum_cores(self, sent):
        return [self.across(self.order(value), -j) for j, value in enumerate(sent, 1)]

    def sum_bits(self, value, bits):
        for bit in bits:
            value = value + self.swap(value, bit)
        return value

    def gather_ordered(self, value):
        return lax.all_gather(
            value, "fsdp", axis=0, tiled=True, axis_index_groups=self.columns
        )

    def reduce_ordered(self, value):
        return lax.psum_scatter(
            value, "fsdp", scatter_dimension=0, tiled=True, axis_index_groups=self.columns
        )

    def stack(self, value, bits):
        stack = value[None]
        for bit in bits:
            stack = jnp.concatenate([stack, self.swap(self.order(stack), bit)], 0)
        return stack


class Rows:
    def __init__(self, groups, rows):
        self.groups, self.rows = groups, groups.order(rows)
        self.one = groups.swap(self.rows, 1)
        self.two = groups.swap(self.rows, 2)

    def middle(self):
        half = self.rows.shape[0] // 2
        self.groups.order.wait(self.one, self.two)
        top, bottom = self.groups.order(self.two[:half], self.one[half:])
        self.top = self.groups.swap(top, 1)
        self.bottom = self.groups.swap(bottom, 2)

    def end(self):
        order = self.groups.order
        order.wait(self.top, self.bottom)
        return jnp.concatenate(
            order(self.rows, self.one, self.two, self.top, self.bottom), 0
        )


class Sums:
    def __init__(self, groups, blocks, late=False):
        self.groups, self.late, blocks = groups, late, groups.order(blocks)
        own, one, two, far = (
            (block[: block.shape[0] // 2], block[block.shape[0] // 2 :])
            for block in jnp.split(blocks, 4)
        )
        self.own, self.one, self.two = own, one, two
        self.far = groups.swap(far[0], 1), groups.swap(far[1], 2)
        if not late:
            self.direct = groups.swap(one[0], 1), groups.swap(two[1], 2)

    def middle(self):
        order, swap = self.groups.order, self.groups.swap
        order.wait(self.far)
        first, second = order(*self.far)
        second = low(high(self.one[1]) + high(second))
        first = low(high(self.two[0]) + high(first))
        if self.late:
            second = jnp.concatenate([self.one[0], second], 0)
            first = jnp.concatenate([first, self.two[1]], 0)
        order.did(first, second)
        first, second = order(first, second)
        self.summed = swap(second, 1), swap(first, 2)

    def end(self):
        order = self.groups.order
        if self.late:
            order.wait(self.summed)
            one, two = order(*self.summed)
            return high(jnp.concatenate(self.own, 0)) + high(one) + high(two)
        order.wait(self.direct, self.summed)
        (one_first, two_second), (one_second, two_first) = order(self.direct, self.summed)
        return jnp.concatenate(
            [
                high(self.own[0]) + high(one_first) + high(two_first),
                high(self.own[1]) + high(one_second) + high(two_second),
            ],
            0,
        )


def after(value, *before):
    return lax.optimization_barrier((value, *before))[0]


def rms_scale(value):
    return lax.rsqrt(jnp.mean(value * value, -1, keepdims=True) + EPS)


def norm_back(value, scale, gain, grad_norm):
    scaled = grad_norm * gain
    return scale * scaled - value * scale**3 * jnp.mean(scaled * value, -1, keepdims=True)


def shift_down(value, places, before):
    return jnp.concatenate([before[:, 2 - places :], value[:, :-places]], 1)


def shift_up(value, places, after):
    return jnp.concatenate([value[:, places:], after[:, :places]], 1)


def on_device(
    tokens,
    seg_ids,
    norm1_gain,
    in_weight,
    conv_weight,
    out_weight,
    norm2_gain,
    gate_weight,
    up_weight,
    down_weight,
    cotangent,
    fsdp,
    tp,
):
    order = Order()
    groups = Groups(fsdp, tp, order)
    deep = groups.deep
    micro_count, own_rows, width = tokens.shape
    rows = micro_count * own_rows
    share = in_weight.shape[2]
    hidden_share = gate_weight.shape[1]
    wide_share = deep * share
    segments = 4 * micro_count
    chip = lax.axis_index("fsdp")
    core = lax.axis_index("tp")

    plane_bits, column_bits, bit = (1, 2), [], 4
    while bit < fsdp:
        column_bits.append(bit)
        bit *= 2

    mixer_own = jnp.concatenate(
        [in_weight.transpose(1, 2, 0).reshape(3 * share, width), out_weight], 0
    )
    mixer_all = groups.gather_ordered(mixer_own)
    pair_own = jnp.concatenate([gate_weight.T, up_weight.T], 0)
    pair_all = groups.gather_ordered(after(pair_own, mixer_own))
    down_all = groups.gather_ordered(after(down_weight, pair_own))

    plane = chip // 4
    same = []
    for places in (1, 2):
        equal = (seg_ids[:, places:] == seg_ids[:, :-places]).astype(jnp.float32)
        equal = jnp.concatenate([jnp.zeros((micro_count, places), jnp.float32), equal], 1)
        same.append(lax.dynamic_slice_in_dim(equal, core * own_rows, own_rows, 1))
    tokens_own = tokens.reshape(rows, width)
    cot_own = cotangent.reshape(rows, width)
    token_rows = Rows(groups, tokens_own)
    gains = groups.stack(jnp.stack([norm1_gain, norm2_gain]), column_bits)
    order.wait(gains, pair_own)
    taps = groups.stack(conv_weight, column_bits)
    order.wait(taps)
    gains = groups.stack(gains, plane_bits[:1])
    same = groups.stack(jnp.stack(same), plane_bits[:1])
    token_rows.middle()
    order.wait(gains, same)
    gains = groups.stack(gains, plane_bits[1:])
    same = groups.stack(same, plane_bits[1:])
    order.wait(gains, same)
    tokens_all = token_rows.end()
    order.did(tokens_all)
    taps = taps[jnp.arange(deep) ^ plane].transpose(1, 0, 2).reshape(3, wide_share)
    taps = [high(tap) for tap in groups.cores(taps)]
    order.wait(taps)
    cot_rows = Rows(groups, cot_own)
    same = same.reshape(4, 2, micro_count, own_rows)
    mask_one = same[:, 0].reshape(segments, own_rows, 1)
    mask_two = same[:, 1].reshape(segments, own_rows, 1)
    gains = gains.reshape(4, deep, 2, -1).swapaxes(0, 1).reshape(fsdp, 2, -1)
    gains = gains[jnp.arange(fsdp) ^ chip].transpose(1, 0, 2).reshape(2, width)
    gain_one = high(gains[0])
    gain_two = high(gains[1])
    tokens_now, gain_now = order(tokens_all, gain_one)
    wide = high(tokens_now)
    scale_all = rms_scale(wide)
    normed = low(wide * scale_all * gain_now)
    order.did(normed)
    cot_rows.middle()
    order.wait(mixer_all)

    mixers = groups.cores(mixer_all)
    in_mats, out_mats, parts, gated_in = [], [], [], []
    for j in range(tp):
        if j:
            order.wait(mixers[j])
        mat = order(mixers[j]).reshape(deep, 4, share, width).transpose(1, 0, 2, 3)
        in_mats.append(mat[:3].reshape(3 * wide_share, width))
        out_mats.append(mat[3].reshape(wide_share, width))
        order.did(in_mats[-1], out_mats[-1])
        normed_now, mat = order(normed, in_mats[-1])
        projected = times_trans(normed_now, mat).reshape(segments, own_rows, 3 * wide_share)
        parts.append([projected[..., k * wide_share : (k + 1) * wide_share] for k in range(3)])
        gated_in.append(parts[-1][1] * parts[-1][2])
        order.did(parts[-1], gated_in[-1])
    ends = groups.next_core(order(jnp.stack([value[:, -2:] for value in gated_in])))
    order.wait(ends)
    parts, gated_in, ends = order(parts, gated_in, ends)
    before = [ends[(j - 1) % tp] for j in range(tp)]
    one_back = [mask_one * shift_down(v, 1, b) for v, b in zip(gated_in, before)]
    two_back = [mask_two * shift_down(v, 2, b) for v, b in zip(gated_in, before)]
    conv_out = [
        tap[0] * v + tap[1] * one + tap[2] * two
        for tap, v, one, two in zip(taps, gated_in, one_back, two_back)
    ]
    mixed = [low(part[0] * out).reshape(4 * rows, -1) for part, out in zip(parts, conv_out)]
    mixer_out = sum_of_products(mixed, out_mats)
    order.did(mixer_out)
    cot_all = cot_rows.end()
    order.wait(cot_all)
    mixer_sums = Sums(groups, mixer_out)
    mixer_sums.middle()
    mixer_sum = mixer_sums.end()
    mixer_sum, tokens_now = order(mixer_sum, tokens_own)
    tokens_f = high(tokens_own)
    resid = high(tokens_now) + mixer_sum

    scale_two = rms_scale(resid)
    normed_own = low(resid * scale_two * gain_two)
    order.did(normed_own)
    two_rows = Rows(groups, normed_own)
    two_rows.middle()
    order.wait(pair_all)
    pairs = groups.cores(pair_all)
    gate, up = [], []
    normed_two = two_rows.end()
    order.did(normed_two)
    hidden, gate_slope, up_slope, grad_gate, grad_up = [], [], [], [], []
    for j in range(tp):
        order.wait(pairs[j])
        pair = order(pairs[j]).reshape(deep, 2, hidden_share, width)
        gate.append(pair[:, 0].reshape(deep * hidden_share, width))
        up.append(pair[:, 1].reshape(deep * hidden_share, width))
        order.did(gate[j], up[j])
        found = ffn_ahead(*order(normed_two, gate[j], up[j]))
        order.did(*found)
        for kept, value in zip((hidden, gate_slope, up_slope), found):
            kept.append(value)

    def core_terms(left, right, flops=1):
        left, right = order(left, right)
        sent = [columns_product(value, right, (), flops) for value in left[1:]]
        order.did(sent)
        return groups.sum_cores(sent)

    def own_term(left, right, got, flops=1, far=True):
        order.wait(got)
        left, right, got = order(left, right, got)
        total = columns_product(left, right, got, flops, far)
        order.did(total)
        return total

    got = core_terms(hidden, cot_all)
    down_total = own_term(hidden[0], cot_all, got)
    order.wait(down_all)
    down_mats = groups.cores(down_all)
    down_grad = groups.reduce_ordered(order(down_total))
    for j in range(tp):
        if j:
            order.wait(down_mats[j])
        found = ffn_back(*order(cot_all, down_mats[j], gate_slope[j], up_slope[j]))
        order.did(*found)
        grad_gate.append(found[0])
        grad_up.append(found[1])
    back_two = sum_of_products(*order(grad_gate + grad_up, gate + up))
    order.did(back_two)
    two_sums = Sums(groups, back_two)
    gate_got = core_terms(grad_gate, normed_two)
    gate_total = own_term(grad_gate[0], normed_two, gate_got)
    two_sums.middle()
    up_got = core_terms(grad_up, normed_two)
    gate_grad = groups.reduce_ordered(order(gate_total))
    up_total = own_term(grad_up[0], normed_two, up_got)
    grad_normed_two = two_sums.end()
    order.wait(down_grad)
    up_grad = groups.reduce_ordered(order(up_total))
    grad_normed_two = order(grad_normed_two)
    resid_back = norm_back(resid, scale_two, gain_two, grad_normed_two)
    grad_resid = high(cot_own) + resid_back
    grad_low = low(grad_resid)
    order.did(grad_low)
    mixer_rows = Rows(groups, grad_low)
    norm_two_term = jnp.sum(grad_normed_two * resid * scale_two, 0)
    hidden_now, down_now = order(hidden, down_mats)
    ffn_out = sum_of_products(hidden_now, down_now)
    order.did(ffn_out, norm_two_term)
    mixer_rows.middle()
    ffn_sums = Sums(groups, ffn_out, True)
    grad_mixer = mixer_rows.end()
    order.did(grad_mixer)

    many = 4 * rows * width * width
    grad_now, mats_now = order(grad_mixer, out_mats)
    grad_mixed = [
        times_trans(grad_now, mat).reshape(segments, own_rows, -1) for mat in mats_now
    ]
    grad_conv = [value * part[0] for value, part in zip(grad_mixed, parts)]
    grad_b = [
        low(value * out).reshape(4 * rows, -1) for value, out in zip(grad_mixed, conv_out)
    ]
    masked_one = [mask_one * value for value in grad_conv]
    masked_two = [mask_two * value for value in grad_conv]
    edges = jnp.stack(
        [jnp.concatenate([one[:, :2], two[:, :2]], 0) for one, two in zip(masked_one, masked_two)]
    )
    order.did(grad_b, grad_conv, edges)
    starts = groups.last_core(order(edges))
    ffn_sums.middle()
    b_got = core_terms(grad_b, normed, many)
    out_got = core_terms(mixed, grad_mixer, many)
    order.wait(starts)
    grad_conv_now, masked_one, masked_two, starts = order(
        grad_conv, masked_one, masked_two, starts
    )
    after_edge = [starts[(j + 1) % tp] for j in range(tp)]
    grad_gated = [
        tap[0] * value
        + tap[1] * shift_up(one, 1, edge[:segments])
        + tap[2] * shift_up(two, 2, edge[segments:])
        for tap, value, one, two, edge in zip(
            taps, grad_conv_now, masked_one, masked_two, after_edge
        )
    ]
    grad_cx = [
        jnp.concatenate([low(gg * part[k]).reshape(4 * rows, -1) for k in (2, 1)], 1)
        for gg, part in zip(grad_gated, parts)
    ]
    order.did(grad_cx)
    cx_got = core_terms(grad_cx, normed, many)
    order.wait(gate_grad)
    b_total = own_term(grad_b[0], normed, b_got, many, False)
    out_total = own_term(mixed[0], grad_mixer, out_got, many, False)
    order.wait(ffn_sums.summed)
    cx_total = own_term(grad_cx[0], normed, cx_got, many, False)
    mixer_total = (
        jnp.concatenate([b_total, cx_total, out_total], 0)
        .reshape(4, deep, share, width)
        .transpose(1, 0, 2, 3)
        .reshape(4 * wide_share, width)
    )
    order.did(mixer_total)
    order.wait(up_grad)
    mixer_grad = groups.reduce_ordered(order(mixer_total))
    block_output = low(resid + ffn_sums.end())
    order.did(block_output)
    b_mats = [mat[:wide_share] for mat in in_mats]
    cx_mats = [mat[wide_share:] for mat in in_mats]
    back_one = sum_of_products(*order(grad_b + grad_cx, b_mats + cx_mats))
    order.did(back_one)
    one_rows = Sums(groups, back_one)
    back_now = order(back_one)
    norm_one_term = jnp.sum(high(back_now) * wide * scale_all, 0)
    conv_terms = [
        jnp.stack([jnp.sum(gc * value, (0, 1)) for value in (gi, one, two)])
        for gc, gi, one, two in zip(grad_conv, gated_in, one_back, two_back)
    ]
    small = [
        jnp.stack(
            [
                norm_one_term,
                norm_two_term,
                jnp.pad(term.reshape(-1), (0, width - 3 * wide_share)),
            ]
        )
        for term in conv_terms
    ]
    order.did(small)
    one_rows.middle()
    small = order(small)
    total = small[0]
    for j in range(1, tp):
        total = total + groups.across(small[j], -j)
    total = groups.sum_bits(total, column_bits)
    order.wait(total)
    grad_normed = one_rows.end()
    input_back = norm_back(tokens_f, rms_scale(tokens_f), gain_one, grad_normed)
    input_grad = low(grad_resid + input_back)
    order.did(input_grad)
    total = order(total)
    conv_total = lax.dynamic_slice_in_dim(
        total[2, : 3 * wide_share].reshape(3, wide_share), plane * share, share, 1
    )
    gain_sums = groups.sum_bits(total[:2], plane_bits)
    gate_grad, up_grad = order(gate_grad, up_grad)
    gate_grad, up_grad = high(gate_grad).T, high(up_grad).T
    order.did(gate_grad, up_grad)
    order.wait(gain_sums)
    order.wait(mixer_grad)
    mixer_grad = order(mixer_grad)
    in_grad = high(mixer_grad[: 3 * share]).reshape(3, share, width)
    out_grad = high(mixer_grad[3 * share :])
    gain_share = norm1_gain.shape[0]
    gain_grads = lax.dynamic_slice_in_dim(gain_sums, chip * gain_share, gain_share, 1)
    return (
        block_output.reshape(tokens.shape),
        input_grad.reshape(tokens.shape),
        gain_grads[0],
        in_grad.transpose(2, 0, 1),
        conv_total,
        out_grad,
        gain_grads[1],
        gate_grad,
        up_grad,
        high(down_grad),
    )


def solution(mesh):
    fsdp, tp = mesh.shape["fsdp"], mesh.shape["tp"]

    def body(*args):
        return on_device(*args, fsdp, tp)

    return jax.shard_map(
        body,
        mesh=mesh,
        in_specs=(
            P(None, ("fsdp", "tp"), None),
            P(None, "fsdp"),
            P("fsdp"),
            P(None, None, ("fsdp", "tp")),
            P(None, ("fsdp", "tp")),
            P(("fsdp", "tp"), None),
            P("fsdp"),
            P(None, ("fsdp", "tp")),
            P(None, ("fsdp", "tp")),
            P(("fsdp", "tp"), None),
            P(None, ("fsdp", "tp"), None),
        ),
        out_specs=(
            P(None, ("fsdp", "tp"), None),
            P(None, ("fsdp", "tp"), None),
            P("fsdp"),
            P(None, None, ("fsdp", "tp")),
            P(None, ("fsdp", "tp")),
            P(("fsdp", "tp"), None),
            P("fsdp"),
            P(None, ("fsdp", "tp")),
            P(None, ("fsdp", "tp")),
            P(("fsdp", "tp"), None),
        ),
        check_vma=False,
    )
```

```python
import jax
import jax.numpy as jnp
from jax import lax
from jax.experimental import pallas as pl
from jax.experimental.pallas import tpu as pltpu
from jax.sharding import PartitionSpec as P

EPS = 1e-05


def matmul(left, right):
    return jnp.dot(left, right, preferred_element_type=jnp.float32)


def times_trans(left, right):
    return lax.dot_general(
        left, right, (((1,), (1,)), ((), ())), preferred_element_type=jnp.float32
    )


def trans_times(left, right):
    return lax.dot_general(
        left, right, (((0,), (0,)), ((), ())), preferred_element_type=jnp.float32
    )


def low(value):
    return value.astype(jnp.bfloat16)


def high(value):
    return value.astype(jnp.float32)


def whole(shape):
    return pl.BlockSpec(shape, lambda i: (0, 0), pipeline_mode=pl.Buffered(1))


def sum_of_products(lefts, rights, tile=256):
    rights = [right if isinstance(right, tuple) else (right, 0) for right in rights]
    offsets = [right[1] for right in rights]
    rights = [right[0] for right in rights]
    rows, width = lefts[0].shape[0], rights[0].shape[1]
    count = len(lefts)
    tile = min(tile, rows)
    depths = [left.shape[1] for left in lefts]
    starts, depth = [], 0
    for size in depths:
        starts.append(depth)
        depth += -(-size // 256) * 256
    limit = 2 * depth * (width + 3 * tile) + 8 * tile * width + 4 * 1024 * 1024

    def body(*refs):
        left_refs, right_refs, out_ref = refs[:count], refs[count : 2 * count], refs[2 * count]
        side, stacked, sems = refs[2 * count + 1 :]
        copies = [
            pltpu.make_async_copy(
                right.at[pl.ds(offset, size)], stacked.at[pl.ds(start, size)], sems.at[k]
            )
            for k, (right, offset, start, size) in enumerate(
                zip(right_refs, offsets, starts, depths)
            )
        ]

        @pl.when(pl.program_id(0) == 0)
        def _():
            for copy in copies:
                copy.start()
            for start, end, size in zip(starts, starts[1:] + [depth], depths):
                if start + size < end:
                    side[:, start + size : end] = jnp.zeros(
                        (tile, end - start - size), jnp.bfloat16
                    )
                    stacked[start + size : end, :] = jnp.zeros(
                        (end - start - size, width), jnp.bfloat16
                    )
            for copy in copies:
                copy.wait()

        for left, start, size in zip(left_refs, starts, depths):
            side[:, start : start + size] = left[...]
        out_ref[...] = low(matmul(side[...], stacked[...]))

    return pl.pallas_call(
        body,
        grid=(rows // tile,),
        in_specs=[pl.BlockSpec((tile, size), lambda i: (i, 0)) for size in depths]
        + [pl.BlockSpec(memory_space=pl.ANY)] * count,
        out_specs=pl.BlockSpec((tile, width), lambda i: (i, 0)),
        out_shape=jax.ShapeDtypeStruct((rows, width), jnp.bfloat16),
        scratch_shapes=[
            pltpu.VMEM((tile, depth), jnp.bfloat16),
            pltpu.VMEM((depth, width), jnp.bfloat16),
            pltpu.SemaphoreType.DMA((count,)),
        ],
        compiler_params=pltpu.CompilerParams(
            dimension_semantics=("arbitrary",), vmem_limit_bytes=limit
        ),
        cost_estimate=pl.CostEstimate(flops=1, bytes_accessed=1, transcendentals=0),
    )(*lefts, *rights)


def rows_product(left, right, tile=256):
    rows, width = left.shape
    count = right.shape[0]
    tile = min(tile, rows)

    def body(left_ref, right_ref, out_ref):
        out_ref[...] = low(times_trans(left_ref[...], right_ref[...]))

    return pl.pallas_call(
        body,
        grid=(rows // tile,),
        in_specs=[pl.BlockSpec((tile, width), lambda i: (i, 0)), whole(right.shape)],
        out_specs=pl.BlockSpec((tile, count), lambda i: (i, 0)),
        out_shape=jax.ShapeDtypeStruct((rows, count), jnp.bfloat16),
        compiler_params=pltpu.CompilerParams(
            dimension_semantics=("arbitrary",), vmem_limit_bytes=12 * 1024 * 1024
        ),
        cost_estimate=pl.CostEstimate(flops=1, bytes_accessed=1, transcendentals=0),
    )(left, right)


def columns_product(left, right, more=(), flops=1, far=False, tile=512):
    rows, count = left.shape
    width = right.shape[1]

    def body(left_ref, right_ref, *refs):
        total = trans_times(left_ref[...], right_ref[...])
        for ref in refs[:-1]:
            total = total + high(ref[...])
        refs[-1][...] = low(total)

    spec = pl.BlockSpec((count, tile), lambda i: (0, i))
    return pl.pallas_call(
        body,
        grid=(width // tile,),
        in_specs=[whole(left.shape), pl.BlockSpec((rows, tile), lambda i: (0, i))]
        + [spec] * len(more),
        out_specs=spec,
        out_shape=(pltpu.HBM if far else jax.ShapeDtypeStruct)((count, width), jnp.bfloat16),
        compiler_params=pltpu.CompilerParams(
            dimension_semantics=("arbitrary",), vmem_limit_bytes=14 * 1024 * 1024
        ),
        cost_estimate=pl.CostEstimate(flops=flops, bytes_accessed=1, transcendentals=0),
    )(left, right, *more)


def ffn_call(body, lefts, rights, slopes, count, tile=256):
    rows, units = lefts[0].shape[0], rights[0].shape[0]
    tile = min(tile, rows)
    spec = pl.BlockSpec((tile, units), lambda i: (i, 0))
    return pl.pallas_call(
        body,
        grid=(rows // tile,),
        in_specs=[pl.BlockSpec((tile, left.shape[1]), lambda i: (i, 0)) for left in lefts]
        + [whole(right.shape) for right in rights]
        + [spec] * len(slopes),
        out_specs=[spec] * count,
        out_shape=[jax.ShapeDtypeStruct((rows, units), jnp.bfloat16)] * count,
        compiler_params=pltpu.CompilerParams(
            dimension_semantics=("arbitrary",), vmem_limit_bytes=20 * 1024 * 1024
        ),
        cost_estimate=pl.CostEstimate(flops=1, bytes_accessed=1, transcendentals=0),
    )(*lefts, *rights, *slopes)


def ffn_ahead(normed, gate, up):
    def body(normed_ref, gate_ref, up_ref, hidden_ref, gate_slope_ref, up_slope_ref):
        pre = times_trans(normed_ref[...], gate_ref[...])
        value = times_trans(normed_ref[...], up_ref[...])
        sigma = jax.nn.sigmoid(pre)
        activated = pre * sigma
        hidden_ref[...] = low(activated * value)
        gate_slope_ref[...] = low(value * sigma * (1.0 + pre * (1.0 - sigma)))
        up_slope_ref[...] = low(activated)

    return ffn_call(body, [normed], [gate, up], [], 3)


def ffn_back(grad, down, gate_slope, up_slope):
    def body(grad_ref, down_ref, gate_slope_ref, up_slope_ref, gate_ref, up_ref):
        grad_hidden = times_trans(grad_ref[...], down_ref[...])
        gate_ref[...] = low(grad_hidden * high(gate_slope_ref[...]))
        up_ref[...] = low(grad_hidden * high(up_slope_ref[...]))

    return ffn_call(body, [grad], [down], [gate_slope, up_slope], 2)


class Order:
    def __init__(self):
        self.last = ()

    def __call__(self, *values):
        values = lax.optimization_barrier((values, self.last))[0]
        return values if len(values) > 1 else values[0]

    def did(self, *results):
        self.last = results

    def wait(self, *results):
        self.last = (*self.last, *results)


class Groups:
    def __init__(self, fsdp, tp, order):
        self.fsdp, self.tp, self.order = fsdp, tp, order
        self.deep = fsdp // 4
        self.columns = [[b + 4 * a for a in range(self.deep)] for b in range(4)]

    def along(self, value):
        pairs = [(i, (i + 4) % self.fsdp) for i in range(self.fsdp)]
        return lax.ppermute(value, "fsdp", pairs)

    def swap(self, value, bit):
        return lax.ppermute(value, "fsdp", [(i, i ^ bit) for i in range(self.fsdp)])

    def across(self, value, places):
        pairs = [(i, (i + places) % self.tp) for i in range(self.tp)]
        return lax.ppermute(value, "tp", pairs)

    def next_core(self, value):
        return lax.ppermute(value, "tp", [(i, i + 1) for i in range(self.tp - 1)])

    def last_core(self, value):
        return lax.ppermute(value, "tp", [(i + 1, i) for i in range(self.tp - 1)])

    def cores(self, value):
        value = self.order(value)
        return [value] + [self.across(value, j) for j in range(1, self.tp)]

    def sum_cores(self, sent):
        return [self.across(self.order(value), -j) for j, value in enumerate(sent, 1)]

    def sum_bits(self, value, bits):
        for bit in bits:
            value = value + self.swap(value, bit)
        return value

    def gather_ordered(self, value):
        return lax.all_gather(
            value, "fsdp", axis=0, tiled=True, axis_index_groups=self.columns
        )

    def reduce_ordered(self, value):
        return lax.psum_scatter(
            value, "fsdp", scatter_dimension=0, tiled=True, axis_index_groups=self.columns
        )

    def stack(self, value, bits):
        stack = value[None]
        for bit in bits:
            stack = jnp.concatenate([stack, self.swap(self.order(stack), bit)], 0)
        return stack


class Rows:
    def __init__(self, groups, rows):
        self.groups, self.rows = groups, groups.order(rows)
        self.one = groups.swap(self.rows, 1)
        self.two = groups.swap(self.rows, 2)

    def middle(self):
        half = self.rows.shape[0] // 2
        self.groups.order.wait(self.one, self.two)
        top, bottom = self.groups.order(self.two[:half], self.one[half:])
        self.top = self.groups.swap(top, 1)
        self.bottom = self.groups.swap(bottom, 2)

    def end(self):
        order = self.groups.order
        order.wait(self.top, self.bottom)
        return jnp.concatenate(
            order(self.rows, self.one, self.two, self.top, self.bottom), 0
        )


class Sums:
    def __init__(self, groups, blocks, late=False):
        self.groups, self.late, blocks = groups, late, groups.order(blocks)
        own, one, two, far = (
            (block[: block.shape[0] // 2], block[block.shape[0] // 2 :])
            for block in jnp.split(blocks, 4)
        )
        self.own, self.one, self.two = own, one, two
        self.far = groups.swap(far[0], 1), groups.swap(far[1], 2)
        if not late:
            self.direct = groups.swap(one[0], 1), groups.swap(two[1], 2)

    def middle(self):
        order, swap = self.groups.order, self.groups.swap
        order.wait(self.far)
        first, second = order(*self.far)
        second = low(high(self.one[1]) + high(second))
        first = low(high(self.two[0]) + high(first))
        if self.late:
            second = jnp.concatenate([self.one[0], second], 0)
            first = jnp.concatenate([first, self.two[1]], 0)
        order.did(first, second)
        first, second = order(first, second)
        self.summed = swap(second, 1), swap(first, 2)

    def end(self):
        order = self.groups.order
        if self.late:
            order.wait(self.summed)
            one, two = order(*self.summed)
            return high(jnp.concatenate(self.own, 0)) + high(one) + high(two)
        order.wait(self.direct, self.summed)
        (one_first, two_second), (one_second, two_first) = order(self.direct, self.summed)
        return jnp.concatenate(
            [
                high(self.own[0]) + high(one_first) + high(two_first),
                high(self.own[1]) + high(one_second) + high(two_second),
            ],
            0,
        )


def after(value, *before):
    return lax.optimization_barrier((value, *before))[0]


def rms_scale(value):
    return lax.rsqrt(jnp.mean(value * value, -1, keepdims=True) + EPS)


def norm_back(value, scale, gain, grad_norm):
    scaled = grad_norm * gain
    return scale * scaled - value * scale**3 * jnp.mean(scaled * value, -1, keepdims=True)


def shift_down(value, places, before):
    return jnp.concatenate([before[:, 2 - places :], value[:, :-places]], 1)


def shift_up(value, places, after):
    return jnp.concatenate([value[:, places:], after[:, :places]], 1)


def on_device(
    tokens,
    seg_ids,
    norm1_gain,
    in_weight,
    conv_weight,
    out_weight,
    norm2_gain,
    gate_weight,
    up_weight,
    down_weight,
    cotangent,
    fsdp,
    tp,
):
    order = Order()
    groups = Groups(fsdp, tp, order)
    deep = groups.deep
    micro_count, own_rows, width = tokens.shape
    rows = micro_count * own_rows
    share = in_weight.shape[2]
    hidden_share = gate_weight.shape[1]
    wide_share = deep * share
    segments = 4 * micro_count
    chip = lax.axis_index("fsdp")
    core = lax.axis_index("tp")

    plane_bits, column_bits, bit = (1, 2), [], 4
    while bit < fsdp:
        column_bits.append(bit)
        bit *= 2

    mixer_own = jnp.concatenate(
        [in_weight.transpose(1, 2, 0).reshape(3 * share, width), out_weight], 0
    )
    mixer_all = groups.gather_ordered(mixer_own)
    pair_own = jnp.concatenate([gate_weight.T, up_weight.T], 0)
    pair_all = groups.gather_ordered(after(pair_own, mixer_own))
    down_all = groups.gather_ordered(after(down_weight, pair_own))

    plane = chip // 4
    same = []
    for places in (1, 2):
        equal = (seg_ids[:, places:] == seg_ids[:, :-places]).astype(jnp.float32)
        equal = jnp.concatenate([jnp.zeros((micro_count, places), jnp.float32), equal], 1)
        same.append(lax.dynamic_slice_in_dim(equal, core * own_rows, own_rows, 1))
    tokens_own = tokens.reshape(rows, width)
    cot_own = cotangent.reshape(rows, width)
    token_rows = Rows(groups, tokens_own)
    gains = groups.stack(jnp.stack([norm1_gain, norm2_gain]), column_bits)
    order.wait(gains, pair_own)
    taps = groups.stack(conv_weight, column_bits)
    order.wait(taps)
    gains = groups.stack(gains, plane_bits[:1])
    same = groups.stack(jnp.stack(same), plane_bits[:1])
    token_rows.middle()
    order.wait(gains, same)
    gains = groups.stack(gains, plane_bits[1:])
    same = groups.stack(same, plane_bits[1:])
    order.wait(gains, same)
    tokens_all = token_rows.end()
    order.did(tokens_all)
    taps = taps[jnp.arange(deep) ^ plane].transpose(1, 0, 2).reshape(3, wide_share)
    taps = [high(tap) for tap in groups.cores(taps)]
    order.wait(taps)
    cot_rows = Rows(groups, cot_own)
    same = same.reshape(4, 2, micro_count, own_rows)
    mask_one = same[:, 0].reshape(segments, own_rows, 1)
    mask_two = same[:, 1].reshape(segments, own_rows, 1)
    gains = gains.reshape(4, deep, 2, -1).swapaxes(0, 1).reshape(fsdp, 2, -1)
    gains = gains[jnp.arange(fsdp) ^ chip].transpose(1, 0, 2).reshape(2, width)
    gain_one = high(gains[0])
    gain_two = high(gains[1])
    tokens_now, gain_now = order(tokens_all, gain_one)
    wide = high(tokens_now)
    scale_all = rms_scale(wide)
    normed = low(wide * scale_all * gain_now)
    order.did(normed)
    cot_rows.middle()
    order.wait(mixer_all)

    mixers = groups.cores(mixer_all)
    in_mats, out_mats, parts, gated_in = [], [], [], []
    for j in range(tp):
        if j:
            order.wait(mixers[j])
        mat = order(mixers[j]).reshape(deep, 4, share, width).transpose(1, 0, 2, 3)
        in_mats.append(mat[:3].reshape(3 * wide_share, width))
        out_mats.append(mat[3].reshape(wide_share, width))
        order.did(in_mats[-1], out_mats[-1])
        normed_now, mat = order(normed, in_mats[-1])
        projected = times_trans(normed_now, mat).reshape(segments, own_rows, 3 * wide_share)
        parts.append([projected[..., k * wide_share : (k + 1) * wide_share] for k in range(3)])
        gated_in.append(parts[-1][1] * parts[-1][2])
        order.did(parts[-1], gated_in[-1])
    ends = groups.next_core(order(jnp.stack([value[:, -2:] for value in gated_in])))
    order.wait(ends)
    parts, gated_in, ends = order(parts, gated_in, ends)
    before = [ends[(j - 1) % tp] for j in range(tp)]
    one_back = [mask_one * shift_down(v, 1, b) for v, b in zip(gated_in, before)]
    two_back = [mask_two * shift_down(v, 2, b) for v, b in zip(gated_in, before)]
    conv_out = [
        tap[0] * v + tap[1] * one + tap[2] * two
        for tap, v, one, two in zip(taps, gated_in, one_back, two_back)
    ]
    mixed = [low(part[0] * out).reshape(4 * rows, -1) for part, out in zip(parts, conv_out)]
    mixer_out = sum_of_products(mixed, out_mats)
    order.did(mixer_out)
    cot_all = cot_rows.end()
    order.wait(cot_all)
    mixer_sums = Sums(groups, mixer_out)
    mixer_sums.middle()
    mixer_sum = mixer_sums.end()
    mixer_sum, tokens_now = order(mixer_sum, tokens_own)
    tokens_f = high(tokens_own)
    resid = high(tokens_now) + mixer_sum

    scale_two = rms_scale(resid)
    normed_own = low(resid * scale_two * gain_two)
    order.did(normed_own)
    two_rows = Rows(groups, normed_own)
    two_rows.middle()
    order.wait(pair_all)
    pairs = groups.cores(pair_all)
    gate, up = [], []
    normed_two = two_rows.end()
    order.did(normed_two)
    hidden, gate_slope, up_slope, grad_gate, grad_up = [], [], [], [], []
    for j in range(tp):
        order.wait(pairs[j])
        pair = order(pairs[j]).reshape(deep, 2, hidden_share, width)
        gate.append(pair[:, 0].reshape(deep * hidden_share, width))
        up.append(pair[:, 1].reshape(deep * hidden_share, width))
        order.did(gate[j], up[j])
        found = ffn_ahead(*order(normed_two, gate[j], up[j]))
        order.did(*found)
        for kept, value in zip((hidden, gate_slope, up_slope), found):
            kept.append(value)

    def core_terms(left, right, flops=1):
        left, right = order(left, right)
        sent = [columns_product(value, right, (), flops) for value in left[1:]]
        order.did(sent)
        return groups.sum_cores(sent)

    def own_term(left, right, got, flops=1, far=True):
        order.wait(got)
        left, right, got = order(left, right, got)
        total = columns_product(left, right, got, flops, far)
        order.did(total)
        return total

    got = core_terms(hidden, cot_all)
    down_total = own_term(hidden[0], cot_all, got)
    order.wait(down_all)
    down_mats = groups.cores(down_all)
    down_grad = groups.reduce_ordered(order(down_total))
    for j in range(tp):
        if j:
            order.wait(down_mats[j])
        found = ffn_back(*order(cot_all, down_mats[j], gate_slope[j], up_slope[j]))
        order.did(*found)
        grad_gate.append(found[0])
        grad_up.append(found[1])
    back_two = sum_of_products(*order(grad_gate + grad_up, gate + up))
    order.did(back_two)
    two_sums = Sums(groups, back_two)
    gate_got = core_terms(grad_gate, normed_two)
    gate_total = own_term(grad_gate[0], normed_two, gate_got)
    two_sums.middle()
    up_got = core_terms(grad_up, normed_two)
    gate_grad = groups.reduce_ordered(order(gate_total))
    up_total = own_term(grad_up[0], normed_two, up_got)
    grad_normed_two = two_sums.end()
    order.wait(down_grad)
    up_grad = groups.reduce_ordered(order(up_total))
    grad_normed_two = order(grad_normed_two)
    resid_back = norm_back(resid, scale_two, gain_two, grad_normed_two)
    grad_resid = high(cot_own) + resid_back
    grad_low = low(grad_resid)
    order.did(grad_low)
    mixer_rows = Rows(groups, grad_low)
    norm_two_term = jnp.sum(grad_normed_two * resid * scale_two, 0)
    hidden_now, down_now = order(hidden, down_mats)
    ffn_out = sum_of_products(hidden_now, down_now)
    order.did(ffn_out, norm_two_term)
    mixer_rows.middle()
    ffn_sums = Sums(groups, ffn_out, True)
    grad_mixer = mixer_rows.end()
    order.did(grad_mixer)

    many = 10**11
    grad_now, mats_now = order(grad_mixer, out_mats)
    grad_mixed = [
        times_trans(grad_now, mat).reshape(segments, own_rows, -1) for mat in mats_now
    ]
    grad_conv = [value * part[0] for value, part in zip(grad_mixed, parts)]
    grad_b = [
        low(value * out).reshape(4 * rows, -1) for value, out in zip(grad_mixed, conv_out)
    ]
    masked_one = [mask_one * value for value in grad_conv]
    masked_two = [mask_two * value for value in grad_conv]
    edges = jnp.stack(
        [jnp.concatenate([one[:, :2], two[:, :2]], 0) for one, two in zip(masked_one, masked_two)]
    )
    order.did(grad_b, grad_conv, edges)
    starts = groups.last_core(order(edges))
    ffn_sums.middle()
    b_got = core_terms(grad_b, normed, many)
    out_got = core_terms(mixed, grad_mixer, many)
    order.wait(starts)
    grad_conv_now, masked_one, masked_two, starts = order(
        grad_conv, masked_one, masked_two, starts
    )
    after_edge = [starts[(j + 1) % tp] for j in range(tp)]
    grad_gated = [
        tap[0] * value
        + tap[1] * shift_up(one, 1, edge[:segments])
        + tap[2] * shift_up(two, 2, edge[segments:])
        for tap, value, one, two, edge in zip(
            taps, grad_conv_now, masked_one, masked_two, after_edge
        )
    ]
    grad_cx = [
        jnp.concatenate([low(gg * part[k]).reshape(4 * rows, -1) for k in (2, 1)], 1)
        for gg, part in zip(grad_gated, parts)
    ]
    order.did(grad_cx)
    cx_got = core_terms(grad_cx, normed, many)
    b_total = own_term(grad_b[0], normed, b_got, many, False)
    out_total = own_term(mixed[0], grad_mixer, out_got, many, False)
    order.wait(gate_grad)
    cx_total = own_term(grad_cx[0], normed, cx_got, many, False)
    mixer_total = (
        jnp.concatenate([b_total, cx_total, out_total], 0)
        .reshape(4, deep, share, width)
        .transpose(1, 0, 2, 3)
        .reshape(4 * wide_share, width)
    )
    order.did(mixer_total)
    order.wait(ffn_sums.summed)
    order.wait(up_grad)
    mixer_grad = groups.reduce_ordered(order(mixer_total))
    grads_now, mats_now = order(grad_b + grad_cx, in_mats)
    cuts = [(mat, start) for start in (0, wide_share) for mat in mats_now]
    back_one = sum_of_products(grads_now, cuts)
    order.did(back_one)
    one_rows = Sums(groups, back_one, True)
    back_now = order(back_one)
    norm_one_term = jnp.sum(high(back_now) * wide * scale_all, 0)
    conv_terms = [
        jnp.stack([jnp.sum(gc * value, (0, 1)) for value in (gi, one, two)])
        for gc, gi, one, two in zip(grad_conv, gated_in, one_back, two_back)
    ]
    small = [
        jnp.stack(
            [
                norm_one_term,
                norm_two_term,
                jnp.pad(term.reshape(-1), (0, width - 3 * wide_share)),
            ]
        )
        for term in conv_terms
    ]
    order.did(small)
    one_rows.middle()
    block_output = low(resid + ffn_sums.end())
    order.did(block_output)
    small = order(small)
    total = small[0]
    for j in range(1, tp):
        total = total + groups.across(small[j], -j)
    total = groups.sum_bits(total, column_bits)
    order.wait(total)
    grad_normed = one_rows.end()
    input_back = norm_back(tokens_f, rms_scale(tokens_f), gain_one, grad_normed)
    input_grad = low(grad_resid + input_back)
    order.did(input_grad)
    total = order(total)
    conv_total = lax.dynamic_slice_in_dim(
        total[2, : 3 * wide_share].reshape(3, wide_share), plane * share, share, 1
    )
    gain_sums = groups.sum_bits(total[:2], plane_bits)
    gate_grad, up_grad = order(gate_grad, up_grad)
    gate_grad, up_grad = high(gate_grad).T, high(up_grad).T
    order.did(gate_grad, up_grad)
    order.wait(gain_sums)
    order.wait(mixer_grad)
    mixer_grad = order(mixer_grad)
    in_grad = high(mixer_grad[: 3 * share]).reshape(3, share, width)
    out_grad = high(mixer_grad[3 * share :])
    gain_share = norm1_gain.shape[0]
    gain_grads = lax.dynamic_slice_in_dim(gain_sums, chip * gain_share, gain_share, 1)
    return (
        block_output.reshape(tokens.shape),
        input_grad.reshape(tokens.shape),
        gain_grads[0],
        in_grad.transpose(2, 0, 1),
        conv_total,
        out_grad,
        gain_grads[1],
        gate_grad,
        up_grad,
        high(down_grad),
    )


def solution(mesh):
    fsdp, tp = mesh.shape["fsdp"], mesh.shape["tp"]

    def body(*args):
        return on_device(*args, fsdp, tp)

    return jax.shard_map(
        body,
        mesh=mesh,
        in_specs=(
            P(None, ("fsdp", "tp"), None),
            P(None, "fsdp"),
            P("fsdp"),
            P(None, None, ("fsdp", "tp")),
            P(None, ("fsdp", "tp")),
            P(("fsdp", "tp"), None),
            P("fsdp"),
            P(None, ("fsdp", "tp")),
            P(None, ("fsdp", "tp")),
            P(("fsdp", "tp"), None),
            P(None, ("fsdp", "tp"), None),
        ),
        out_specs=(
            P(None, ("fsdp", "tp"), None),
            P(None, ("fsdp", "tp"), None),
            P("fsdp"),
            P(None, None, ("fsdp", "tp")),
            P(None, ("fsdp", "tp")),
            P(("fsdp", "tp"), None),
            P("fsdp"),
            P(None, ("fsdp", "tp")),
            P(None, ("fsdp", "tp")),
            P(("fsdp", "tp"), None),
        ),
        check_vma=False,
    )
```

```python
import jax
import jax.numpy as jnp
from jax import lax
from jax.experimental import pallas as pl
from jax.experimental.pallas import tpu as pltpu
from jax.sharding import PartitionSpec as P

EPS = 1e-05


def matmul(left, right):
    return jnp.dot(left, right, preferred_element_type=jnp.float32)


def times_trans(left, right):
    return lax.dot_general(
        left, right, (((1,), (1,)), ((), ())), preferred_element_type=jnp.float32
    )


def trans_times(left, right):
    return lax.dot_general(
        left, right, (((0,), (0,)), ((), ())), preferred_element_type=jnp.float32
    )


def low(value):
    return value.astype(jnp.bfloat16)


def high(value):
    return value.astype(jnp.float32)


def whole(shape):
    return pl.BlockSpec(shape, lambda i: (0, 0), pipeline_mode=pl.Buffered(1))


def sum_of_products(lefts, rights, tile=256):
    rights = [right if isinstance(right, tuple) else (right, 0) for right in rights]
    offsets = [right[1] for right in rights]
    rights = [right[0] for right in rights]
    rows, width = lefts[0].shape[0], rights[0].shape[1]
    count = len(lefts)
    tile = min(tile, rows)
    depths = [left.shape[1] for left in lefts]
    starts, depth = [], 0
    for size in depths:
        starts.append(depth)
        depth += -(-size // 256) * 256
    limit = 2 * depth * (width + 3 * tile) + 8 * tile * width + 4 * 1024 * 1024

    def body(*refs):
        left_refs, right_refs, out_ref = refs[:count], refs[count : 2 * count], refs[2 * count]
        side, stacked, sems = refs[2 * count + 1 :]
        copies = [
            pltpu.make_async_copy(
                right.at[pl.ds(offset, size)], stacked.at[pl.ds(start, size)], sems.at[k]
            )
            for k, (right, offset, start, size) in enumerate(
                zip(right_refs, offsets, starts, depths)
            )
        ]

        @pl.when(pl.program_id(0) == 0)
        def _():
            for copy in copies:
                copy.start()
            for start, end, size in zip(starts, starts[1:] + [depth], depths):
                if start + size < end:
                    side[:, start + size : end] = jnp.zeros(
                        (tile, end - start - size), jnp.bfloat16
                    )
                    stacked[start + size : end, :] = jnp.zeros(
                        (end - start - size, width), jnp.bfloat16
                    )
            for copy in copies:
                copy.wait()

        for left, start, size in zip(left_refs, starts, depths):
            side[:, start : start + size] = left[...]
        out_ref[...] = low(matmul(side[...], stacked[...]))

    return pl.pallas_call(
        body,
        grid=(rows // tile,),
        in_specs=[pl.BlockSpec((tile, size), lambda i: (i, 0)) for size in depths]
        + [pl.BlockSpec(memory_space=pl.ANY)] * count,
        out_specs=pl.BlockSpec((tile, width), lambda i: (i, 0)),
        out_shape=jax.ShapeDtypeStruct((rows, width), jnp.bfloat16),
        scratch_shapes=[
            pltpu.VMEM((tile, depth), jnp.bfloat16),
            pltpu.VMEM((depth, width), jnp.bfloat16),
            pltpu.SemaphoreType.DMA((count,)),
        ],
        compiler_params=pltpu.CompilerParams(
            dimension_semantics=("arbitrary",), vmem_limit_bytes=limit
        ),
        cost_estimate=pl.CostEstimate(flops=1, bytes_accessed=1, transcendentals=0),
    )(*lefts, *rights)


def rows_product(left, right, tile=256):
    rows, width = left.shape
    count = right.shape[0]
    tile = min(tile, rows)

    def body(left_ref, right_ref, out_ref):
        out_ref[...] = low(times_trans(left_ref[...], right_ref[...]))

    return pl.pallas_call(
        body,
        grid=(rows // tile,),
        in_specs=[pl.BlockSpec((tile, width), lambda i: (i, 0)), whole(right.shape)],
        out_specs=pl.BlockSpec((tile, count), lambda i: (i, 0)),
        out_shape=jax.ShapeDtypeStruct((rows, count), jnp.bfloat16),
        compiler_params=pltpu.CompilerParams(
            dimension_semantics=("arbitrary",), vmem_limit_bytes=12 * 1024 * 1024
        ),
        cost_estimate=pl.CostEstimate(flops=1, bytes_accessed=1, transcendentals=0),
    )(left, right)


def columns_product(left, right, more=(), flops=1, far=False, tile=512):
    rows, count = left.shape
    width = right.shape[1]

    def body(left_ref, right_ref, *refs):
        total = trans_times(left_ref[...], right_ref[...])
        for ref in refs[:-1]:
            total = total + high(ref[...])
        refs[-1][...] = low(total)

    spec = pl.BlockSpec((count, tile), lambda i: (0, i))
    return pl.pallas_call(
        body,
        grid=(width // tile,),
        in_specs=[whole(left.shape), pl.BlockSpec((rows, tile), lambda i: (0, i))]
        + [spec] * len(more),
        out_specs=spec,
        out_shape=(pltpu.HBM if far else jax.ShapeDtypeStruct)((count, width), jnp.bfloat16),
        compiler_params=pltpu.CompilerParams(
            dimension_semantics=("arbitrary",), vmem_limit_bytes=14 * 1024 * 1024
        ),
        cost_estimate=pl.CostEstimate(flops=flops, bytes_accessed=1, transcendentals=0),
    )(left, right, *more)


def mixer_product(left, right, more, first, last, deep, flops, tile=512):
    rows, count = left.shape
    width = right.shape[1]
    wide = first.shape[0]
    share, parts = wide // deep, count // wide

    def body(left_ref, right_ref, first_ref, last_ref, *refs):
        total = trans_times(left_ref[...], right_ref[...])
        for ref in refs[:-1]:
            total = total + high(ref[...])
        total = low(total)
        for plane in range(deep):
            own = slice(plane * share, (plane + 1) * share)
            refs[-1][plane, 0] = first_ref[own, :]
            for k in range(parts):
                refs[-1][plane, 1 + k] = total[k * wide + own.start : k * wide + own.stop]
            refs[-1][plane, 1 + parts] = last_ref[own, :]

    def columns(size):
        return pl.BlockSpec((size, tile), lambda i: (0, i))

    return pl.pallas_call(
        body,
        grid=(width // tile,),
        in_specs=[whole(left.shape), columns(rows), columns(wide), columns(wide)]
        + [columns(count)] * len(more),
        out_specs=pl.BlockSpec((deep, 2 + parts, share, tile), lambda i: (0, 0, 0, i)),
        out_shape=pltpu.HBM((deep, 2 + parts, share, width), jnp.bfloat16),
        compiler_params=pltpu.CompilerParams(
            dimension_semantics=("arbitrary",), vmem_limit_bytes=16 * 1024 * 1024
        ),
        cost_estimate=pl.CostEstimate(flops=flops, bytes_accessed=1, transcendentals=0),
    )(left, right, first, last, *more)


def ffn_call(body, lefts, rights, slopes, count, tile=256):
    rows, units = lefts[0].shape[0], rights[0].shape[0]
    tile = min(tile, rows)
    spec = pl.BlockSpec((tile, units), lambda i: (i, 0))
    return pl.pallas_call(
        body,
        grid=(rows // tile,),
        in_specs=[pl.BlockSpec((tile, left.shape[1]), lambda i: (i, 0)) for left in lefts]
        + [whole(right.shape) for right in rights]
        + [spec] * len(slopes),
        out_specs=[spec] * count,
        out_shape=[jax.ShapeDtypeStruct((rows, units), jnp.bfloat16)] * count,
        compiler_params=pltpu.CompilerParams(
            dimension_semantics=("arbitrary",), vmem_limit_bytes=20 * 1024 * 1024
        ),
        cost_estimate=pl.CostEstimate(flops=1, bytes_accessed=1, transcendentals=0),
    )(*lefts, *rights, *slopes)


def ffn_ahead(normed, gate, up):
    def body(normed_ref, gate_ref, up_ref, hidden_ref, gate_slope_ref, up_slope_ref):
        pre = times_trans(normed_ref[...], gate_ref[...])
        value = times_trans(normed_ref[...], up_ref[...])
        sigma = jax.nn.sigmoid(pre)
        activated = pre * sigma
        hidden_ref[...] = low(activated * value)
        gate_slope_ref[...] = low(value * sigma * (1.0 + pre * (1.0 - sigma)))
        up_slope_ref[...] = low(activated)

    return ffn_call(body, [normed], [gate, up], [], 3)


def ffn_back(grad, down, gate_slope, up_slope):
    def body(grad_ref, down_ref, gate_slope_ref, up_slope_ref, gate_ref, up_ref):
        grad_hidden = times_trans(grad_ref[...], down_ref[...])
        gate_ref[...] = low(grad_hidden * high(gate_slope_ref[...]))
        up_ref[...] = low(grad_hidden * high(up_slope_ref[...]))

    return ffn_call(body, [grad], [down], [gate_slope, up_slope], 2)


class Order:
    def __init__(self):
        self.last = ()

    def __call__(self, *values):
        values = lax.optimization_barrier((values, self.last))[0]
        return values if len(values) > 1 else values[0]

    def did(self, *results):
        self.last = results

    def wait(self, *results):
        self.last = (*self.last, *results)


class Groups:
    def __init__(self, fsdp, tp, order):
        self.fsdp, self.tp, self.order = fsdp, tp, order
        self.deep = fsdp // 4
        self.columns = [[b + 4 * a for a in range(self.deep)] for b in range(4)]

    def along(self, value):
        pairs = [(i, (i + 4) % self.fsdp) for i in range(self.fsdp)]
        return lax.ppermute(value, "fsdp", pairs)

    def swap(self, value, bit):
        return lax.ppermute(value, "fsdp", [(i, i ^ bit) for i in range(self.fsdp)])

    def across(self, value, places):
        pairs = [(i, (i + places) % self.tp) for i in range(self.tp)]
        return lax.ppermute(value, "tp", pairs)

    def next_core(self, value):
        return lax.ppermute(value, "tp", [(i, i + 1) for i in range(self.tp - 1)])

    def last_core(self, value):
        return lax.ppermute(value, "tp", [(i + 1, i) for i in range(self.tp - 1)])

    def cores(self, value):
        value = self.order(value)
        return [value] + [self.across(value, j) for j in range(1, self.tp)]

    def sum_cores(self, sent):
        return [self.across(self.order(value), -j) for j, value in enumerate(sent, 1)]

    def sum_bits(self, value, bits):
        for bit in bits:
            value = value + self.swap(value, bit)
        return value

    def gather_ordered(self, value):
        return lax.all_gather(
            value, "fsdp", axis=0, tiled=True, axis_index_groups=self.columns
        )

    def reduce_ordered(self, value):
        return lax.psum_scatter(
            value, "fsdp", scatter_dimension=0, tiled=True, axis_index_groups=self.columns
        )

    def stack(self, value, bits):
        stack = value[None]
        for bit in bits:
            stack = jnp.concatenate([stack, self.swap(self.order(stack), bit)], 0)
        return stack


class Rows:
    def __init__(self, groups, rows):
        self.groups, self.rows = groups, groups.order(rows)
        self.one = groups.swap(self.rows, 1)
        self.two = groups.swap(self.rows, 2)

    def middle(self):
        half = self.rows.shape[0] // 2
        self.groups.order.wait(self.one, self.two)
        top, bottom = self.groups.order(self.two[:half], self.one[half:])
        self.top = self.groups.swap(top, 1)
        self.bottom = self.groups.swap(bottom, 2)

    def end(self):
        order = self.groups.order
        order.wait(self.top, self.bottom)
        return jnp.concatenate(
            order(self.rows, self.one, self.two, self.top, self.bottom), 0
        )


class Sums:
    def __init__(self, groups, blocks, late=False):
        self.groups, self.late, blocks = groups, late, groups.order(blocks)
        own, one, two, far = (
            (block[: block.shape[0] // 2], block[block.shape[0] // 2 :])
            for block in jnp.split(blocks, 4)
        )
        self.own, self.one, self.two = own, one, two
        self.far = groups.swap(far[0], 1), groups.swap(far[1], 2)
        if not late:
            self.direct = groups.swap(one[0], 1), groups.swap(two[1], 2)

    def middle(self):
        order, swap = self.groups.order, self.groups.swap
        order.wait(self.far)
        first, second = order(*self.far)
        second = low(high(self.one[1]) + high(second))
        first = low(high(self.two[0]) + high(first))
        if self.late:
            second = jnp.concatenate([self.one[0], second], 0)
            first = jnp.concatenate([first, self.two[1]], 0)
        order.did(first, second)
        first, second = order(first, second)
        self.summed = swap(second, 1), swap(first, 2)

    def end(self):
        order = self.groups.order
        if self.late:
            order.wait(self.summed)
            one, two = order(*self.summed)
            return high(jnp.concatenate(self.own, 0)) + high(one) + high(two)
        order.wait(self.direct, self.summed)
        (one_first, two_second), (one_second, two_first) = order(self.direct, self.summed)
        return jnp.concatenate(
            [
                high(self.own[0]) + high(one_first) + high(two_first),
                high(self.own[1]) + high(one_second) + high(two_second),
            ],
            0,
        )


def after(value, *before):
    return lax.optimization_barrier((value, *before))[0]


def rms_scale(value):
    return lax.rsqrt(jnp.mean(value * value, -1, keepdims=True) + EPS)


def norm_back(value, scale, gain, grad_norm):
    scaled = grad_norm * gain
    return scale * scaled - value * scale**3 * jnp.mean(scaled * value, -1, keepdims=True)


def shift_down(value, places, before):
    return jnp.concatenate([before[:, 2 - places :], value[:, :-places]], 1)


def shift_up(value, places, after):
    return jnp.concatenate([value[:, places:], after[:, :places]], 1)


def on_device(
    tokens,
    seg_ids,
    norm1_gain,
    in_weight,
    conv_weight,
    out_weight,
    norm2_gain,
    gate_weight,
    up_weight,
    down_weight,
    cotangent,
    fsdp,
    tp,
):
    order = Order()
    groups = Groups(fsdp, tp, order)
    deep = groups.deep
    micro_count, own_rows, width = tokens.shape
    rows = micro_count * own_rows
    share = in_weight.shape[2]
    hidden_share = gate_weight.shape[1]
    wide_share = deep * share
    segments = 4 * micro_count
    chip = lax.axis_index("fsdp")
    core = lax.axis_index("tp")

    plane_bits, column_bits, bit = (1, 2), [], 4
    while bit < fsdp:
        column_bits.append(bit)
        bit *= 2

    mixer_own = jnp.concatenate(
        [in_weight.transpose(1, 2, 0).reshape(3 * share, width), out_weight], 0
    )
    mixer_all = groups.gather_ordered(mixer_own)
    pair_own = jnp.concatenate([gate_weight.T, up_weight.T], 0)
    pair_all = groups.gather_ordered(after(pair_own, mixer_own))
    down_all = groups.gather_ordered(after(down_weight, pair_own))

    plane = chip // 4
    same = []
    for places in (1, 2):
        equal = (seg_ids[:, places:] == seg_ids[:, :-places]).astype(jnp.float32)
        equal = jnp.concatenate([jnp.zeros((micro_count, places), jnp.float32), equal], 1)
        same.append(lax.dynamic_slice_in_dim(equal, core * own_rows, own_rows, 1))
    tokens_own = tokens.reshape(rows, width)
    cot_own = cotangent.reshape(rows, width)
    token_rows = Rows(groups, tokens_own)
    gains = groups.stack(jnp.stack([norm1_gain, norm2_gain]), column_bits)
    order.wait(gains, pair_own)
    taps = groups.stack(conv_weight, column_bits)
    order.wait(taps)
    gains = groups.stack(gains, plane_bits[:1])
    same = groups.stack(jnp.stack(same), plane_bits[:1])
    token_rows.middle()
    order.wait(gains, same)
    gains = groups.stack(gains, plane_bits[1:])
    same = groups.stack(same, plane_bits[1:])
    order.wait(gains, same)
    tokens_all = token_rows.end()
    order.did(tokens_all)
    taps = taps[jnp.arange(deep) ^ plane].transpose(1, 0, 2).reshape(3, wide_share)
    taps = [high(tap) for tap in groups.cores(taps)]
    order.wait(taps)
    cot_rows = Rows(groups, cot_own)
    same = same.reshape(4, 2, micro_count, own_rows)
    mask_one = same[:, 0].reshape(segments, own_rows, 1)
    mask_two = same[:, 1].reshape(segments, own_rows, 1)
    gains = gains.reshape(4, deep, 2, -1).swapaxes(0, 1).reshape(fsdp, 2, -1)
    gains = gains[jnp.arange(fsdp) ^ chip].transpose(1, 0, 2).reshape(2, width)
    gain_one = high(gains[0])
    gain_two = high(gains[1])
    tokens_now, gain_now = order(tokens_all, gain_one)
    wide = high(tokens_now)
    scale_all = rms_scale(wide)
    normed = low(wide * scale_all * gain_now)
    order.did(normed)
    cot_rows.middle()
    order.wait(mixer_all)

    mixers = groups.cores(mixer_all)
    in_mats, out_mats, parts, gated_in = [], [], [], []
    for j in range(tp):
        if j:
            order.wait(mixers[j])
        mat = order(mixers[j]).reshape(deep, 4, share, width).transpose(1, 0, 2, 3)
        in_mats.append(mat[:3].reshape(3 * wide_share, width))
        out_mats.append(mat[3].reshape(wide_share, width))
        order.did(in_mats[-1], out_mats[-1])
        normed_now, mat = order(normed, in_mats[-1])
        projected = times_trans(normed_now, mat).reshape(segments, own_rows, 3 * wide_share)
        parts.append([projected[..., k * wide_share : (k + 1) * wide_share] for k in range(3)])
        gated_in.append(parts[-1][1] * parts[-1][2])
        order.did(parts[-1], gated_in[-1])
    ends = groups.next_core(order(jnp.stack([value[:, -2:] for value in gated_in])))
    order.wait(ends)
    parts, gated_in, ends = order(parts, gated_in, ends)
    before = [ends[(j - 1) % tp] for j in range(tp)]
    one_back = [mask_one * shift_down(v, 1, b) for v, b in zip(gated_in, before)]
    two_back = [mask_two * shift_down(v, 2, b) for v, b in zip(gated_in, before)]
    conv_out = [
        tap[0] * v + tap[1] * one + tap[2] * two
        for tap, v, one, two in zip(taps, gated_in, one_back, two_back)
    ]
    mixed = [low(part[0] * out).reshape(4 * rows, -1) for part, out in zip(parts, conv_out)]
    mixer_out = sum_of_products(mixed, out_mats)
    order.did(mixer_out)
    cot_all = cot_rows.end()
    order.wait(cot_all)
    mixer_sums = Sums(groups, mixer_out, True)
    mixer_sums.middle()
    mixer_sum = mixer_sums.end()
    mixer_sum, tokens_now = order(mixer_sum, tokens_own)
    tokens_f = high(tokens_own)
    resid = high(tokens_now) + mixer_sum

    scale_two = rms_scale(resid)
    normed_own = low(resid * scale_two * gain_two)
    order.did(normed_own)
    two_rows = Rows(groups, normed_own)
    two_rows.middle()
    order.wait(pair_all)
    pairs = groups.cores(pair_all)
    gate, up = [], []
    normed_two = two_rows.end()
    order.did(normed_two)
    hidden, gate_slope, up_slope, grad_gate, grad_up = [], [], [], [], []
    for j in range(tp):
        order.wait(pairs[j])
        pair = order(pairs[j]).reshape(deep, 2, hidden_share, width)
        gate.append(pair[:, 0].reshape(deep * hidden_share, width))
        up.append(pair[:, 1].reshape(deep * hidden_share, width))
        order.did(gate[j], up[j])
        found = ffn_ahead(*order(normed_two, gate[j], up[j]))
        order.did(*found)
        for kept, value in zip((hidden, gate_slope, up_slope), found):
            kept.append(value)

    def core_terms(left, right, flops=1):
        left, right = order(left, right)
        sent = [columns_product(value, right, (), flops) for value in left[1:]]
        order.did(sent)
        return groups.sum_cores(sent)

    def own_term(left, right, got, flops=1, far=True):
        order.wait(got)
        left, right, got = order(left, right, got)
        total = columns_product(left, right, got, flops, far)
        order.did(total)
        return total

    got = core_terms(hidden, cot_all)
    down_total = own_term(hidden[0], cot_all, got)
    order.wait(down_all)
    down_mats = groups.cores(down_all)
    down_grad = groups.reduce_ordered(order(down_total))
    for j in range(tp):
        if j:
            order.wait(down_mats[j])
        found = ffn_back(*order(cot_all, down_mats[j], gate_slope[j], up_slope[j]))
        order.did(*found)
        grad_gate.append(found[0])
        grad_up.append(found[1])
    back_two = sum_of_products(*order(grad_gate + grad_up, gate + up))
    order.did(back_two)
    two_sums = Sums(groups, back_two, True)
    gate_got = core_terms(grad_gate, normed_two)
    gate_total = own_term(grad_gate[0], normed_two, gate_got)
    two_sums.middle()
    up_got = core_terms(grad_up, normed_two)
    gate_grad = groups.reduce_ordered(order(gate_total))
    up_total = own_term(grad_up[0], normed_two, up_got)
    grad_normed_two = two_sums.end()
    order.wait(down_grad)
    up_grad = groups.reduce_ordered(order(up_total))
    grad_normed_two = order(grad_normed_two)
    resid_back = norm_back(resid, scale_two, gain_two, grad_normed_two)
    grad_resid = high(cot_own) + resid_back
    grad_low = low(grad_resid)
    order.did(grad_low)
    mixer_rows = Rows(groups, grad_low)
    norm_two_term = jnp.sum(grad_normed_two * resid * scale_two, 0)
    hidden_now, down_now = order(hidden, down_mats)
    ffn_out = sum_of_products(hidden_now, down_now)
    order.did(ffn_out, norm_two_term)
    mixer_rows.middle()
    ffn_sums = Sums(groups, ffn_out, True)
    grad_mixer = mixer_rows.end()
    order.did(grad_mixer)

    many = 10**11
    grad_now, mats_now = order(grad_mixer, out_mats)
    grad_mixed = [
        times_trans(grad_now, mat).reshape(segments, own_rows, -1) for mat in mats_now
    ]
    grad_conv = [value * part[0] for value, part in zip(grad_mixed, parts)]
    grad_b = [
        low(value * out).reshape(4 * rows, -1) for value, out in zip(grad_mixed, conv_out)
    ]
    masked_one = [mask_one * value for value in grad_conv]
    masked_two = [mask_two * value for value in grad_conv]
    edges = jnp.stack(
        [jnp.concatenate([one[:, :2], two[:, :2]], 0) for one, two in zip(masked_one, masked_two)]
    )
    order.did(grad_b, grad_conv, edges)
    starts = groups.last_core(order(edges))
    ffn_sums.middle()
    b_got = core_terms(grad_b, normed, many)
    out_got = core_terms(mixed, grad_mixer, many)
    order.wait(starts)
    grad_conv_now, masked_one, masked_two, starts = order(
        grad_conv, masked_one, masked_two, starts
    )
    after_edge = [starts[(j + 1) % tp] for j in range(tp)]
    grad_gated = [
        tap[0] * value
        + tap[1] * shift_up(one, 1, edge[:segments])
        + tap[2] * shift_up(two, 2, edge[segments:])
        for tap, value, one, two, edge in zip(
            taps, grad_conv_now, masked_one, masked_two, after_edge
        )
    ]
    grad_cx = [
        jnp.concatenate([low(gg * part[k]).reshape(4 * rows, -1) for k in (2, 1)], 1)
        for gg, part in zip(grad_gated, parts)
    ]
    order.did(grad_cx)
    cx_got = core_terms(grad_cx, normed, many)
    b_total = own_term(grad_b[0], normed, b_got, many, False)
    out_total = own_term(mixed[0], grad_mixer, out_got, many, False)
    order.wait(gate_grad)
    order.wait(cx_got)
    mixer_total = mixer_product(
        *order(grad_cx[0], normed, cx_got, b_total, out_total), deep, many
    ).reshape(4 * wide_share, width)
    order.did(mixer_total)
    order.wait(ffn_sums.summed)
    order.wait(up_grad)
    mixer_grad = groups.reduce_ordered(order(mixer_total))
    grads_now, mats_now = order(grad_b + grad_cx, in_mats)
    cuts = [(mat, start) for start in (0, wide_share) for mat in mats_now]
    back_one = sum_of_products(grads_now, cuts)
    order.did(back_one)
    one_rows = Sums(groups, back_one, True)
    back_now = order(back_one)
    norm_one_term = jnp.sum(high(back_now) * wide * scale_all, 0)
    conv_terms = [
        jnp.stack([jnp.sum(gc * value, (0, 1)) for value in (gi, one, two)])
        for gc, gi, one, two in zip(grad_conv, gated_in, one_back, two_back)
    ]
    small = [
        jnp.stack(
            [
                norm_one_term,
                norm_two_term,
                jnp.pad(term.reshape(-1), (0, width - 3 * wide_share)),
            ]
        )
        for term in conv_terms
    ]
    order.did(small)
    one_rows.middle()
    block_output = low(resid + ffn_sums.end())
    order.did(block_output)
    small = order(small)
    total = small[0]
    for j in range(1, tp):
        total = total + groups.across(small[j], -j)
    total = groups.sum_bits(total, column_bits)
    order.wait(total)
    grad_normed = one_rows.end()
    input_back = norm_back(tokens_f, rms_scale(tokens_f), gain_one, grad_normed)
    input_grad = low(grad_resid + input_back)
    order.did(input_grad)
    total = order(total)
    conv_total = lax.dynamic_slice_in_dim(
        total[2, : 3 * wide_share].reshape(3, wide_share), plane * share, share, 1
    )
    gain_sums = groups.sum_bits(total[:2], plane_bits)
    gate_grad, up_grad = order(gate_grad, up_grad)
    gate_grad, up_grad = high(gate_grad).T, high(up_grad).T
    order.did(gate_grad, up_grad)
    order.wait(gain_sums)
    order.wait(mixer_grad)
    mixer_grad = order(mixer_grad)
    in_grad = high(mixer_grad[: 3 * share]).reshape(3, share, width)
    out_grad = high(mixer_grad[3 * share :])
    gain_share = norm1_gain.shape[0]
    gain_grads = lax.dynamic_slice_in_dim(gain_sums, chip * gain_share, gain_share, 1)
    return (
        block_output.reshape(tokens.shape),
        input_grad.reshape(tokens.shape),
        gain_grads[0],
        in_grad.transpose(2, 0, 1),
        conv_total,
        out_grad,
        gain_grads[1],
        gate_grad,
        up_grad,
        high(down_grad),
    )


def solution(mesh):
    fsdp, tp = mesh.shape["fsdp"], mesh.shape["tp"]

    def body(*args):
        return on_device(*args, fsdp, tp)

    return jax.shard_map(
        body,
        mesh=mesh,
        in_specs=(
            P(None, ("fsdp", "tp"), None),
            P(None, "fsdp"),
            P("fsdp"),
            P(None, None, ("fsdp", "tp")),
            P(None, ("fsdp", "tp")),
            P(("fsdp", "tp"), None),
            P("fsdp"),
            P(None, ("fsdp", "tp")),
            P(None, ("fsdp", "tp")),
            P(("fsdp", "tp"), None),
            P(None, ("fsdp", "tp"), None),
        ),
        out_specs=(
            P(None, ("fsdp", "tp"), None),
            P(None, ("fsdp", "tp"), None),
            P("fsdp"),
            P(None, None, ("fsdp", "tp")),
            P(None, ("fsdp", "tp")),
            P(("fsdp", "tp"), None),
            P("fsdp"),
            P(None, ("fsdp", "tp")),
            P(None, ("fsdp", "tp")),
            P(("fsdp", "tp"), None),
        ),
        check_vma=False,
    )
```

```python
import jax
import jax.numpy as jnp
from jax import lax
from jax.experimental import pallas as pl
from jax.experimental.pallas import tpu as pltpu
from jax.sharding import PartitionSpec as P

EPS = 1e-05


def matmul(left, right):
    return jnp.dot(left, right, preferred_element_type=jnp.float32)


def times_trans(left, right):
    return lax.dot_general(
        left, right, (((1,), (1,)), ((), ())), preferred_element_type=jnp.float32
    )


def trans_times(left, right):
    return lax.dot_general(
        left, right, (((0,), (0,)), ((), ())), preferred_element_type=jnp.float32
    )


def low(value):
    return value.astype(jnp.bfloat16)


def high(value):
    return value.astype(jnp.float32)


def whole(shape):
    return pl.BlockSpec(shape, lambda i: (0, 0), pipeline_mode=pl.Buffered(1))


def sum_of_products(lefts, rights, tile=256):
    rights = [right if isinstance(right, tuple) else (right, 0) for right in rights]
    offsets = [right[1] for right in rights]
    rights = [right[0] for right in rights]
    rows, width = lefts[0].shape[0], rights[0].shape[1]
    count = len(lefts)
    tile = min(tile, rows)
    depths = [left.shape[1] for left in lefts]
    starts, depth = [], 0
    for size in depths:
        starts.append(depth)
        depth += -(-size // 256) * 256
    limit = 2 * depth * (width + 3 * tile) + 8 * tile * width + 4 * 1024 * 1024

    def body(*refs):
        left_refs, right_refs, out_ref = refs[:count], refs[count : 2 * count], refs[2 * count]
        side, stacked, sems = refs[2 * count + 1 :]
        copies = [
            pltpu.make_async_copy(
                right.at[pl.ds(offset, size)], stacked.at[pl.ds(start, size)], sems.at[k]
            )
            for k, (right, offset, start, size) in enumerate(
                zip(right_refs, offsets, starts, depths)
            )
        ]

        @pl.when(pl.program_id(0) == 0)
        def _():
            for copy in copies:
                copy.start()
            for start, end, size in zip(starts, starts[1:] + [depth], depths):
                if start + size < end:
                    side[:, start + size : end] = jnp.zeros(
                        (tile, end - start - size), jnp.bfloat16
                    )
                    stacked[start + size : end, :] = jnp.zeros(
                        (end - start - size, width), jnp.bfloat16
                    )
            for copy in copies:
                copy.wait()

        for left, start, size in zip(left_refs, starts, depths):
            side[:, start : start + size] = left[...]
        out_ref[...] = low(matmul(side[...], stacked[...]))

    return pl.pallas_call(
        body,
        grid=(rows // tile,),
        in_specs=[pl.BlockSpec((tile, size), lambda i: (i, 0)) for size in depths]
        + [pl.BlockSpec(memory_space=pl.ANY)] * count,
        out_specs=pl.BlockSpec((tile, width), lambda i: (i, 0)),
        out_shape=jax.ShapeDtypeStruct((rows, width), jnp.bfloat16),
        scratch_shapes=[
            pltpu.VMEM((tile, depth), jnp.bfloat16),
            pltpu.VMEM((depth, width), jnp.bfloat16),
            pltpu.SemaphoreType.DMA((count,)),
        ],
        compiler_params=pltpu.CompilerParams(
            dimension_semantics=("arbitrary",), vmem_limit_bytes=limit
        ),
        cost_estimate=pl.CostEstimate(flops=1, bytes_accessed=1, transcendentals=0),
    )(*lefts, *rights)


def rows_product(left, right, tile=256):
    rows, width = left.shape
    count = right.shape[0]
    tile = min(tile, rows)

    def body(left_ref, right_ref, out_ref):
        out_ref[...] = low(times_trans(left_ref[...], right_ref[...]))

    return pl.pallas_call(
        body,
        grid=(rows // tile,),
        in_specs=[pl.BlockSpec((tile, width), lambda i: (i, 0)), whole(right.shape)],
        out_specs=pl.BlockSpec((tile, count), lambda i: (i, 0)),
        out_shape=jax.ShapeDtypeStruct((rows, count), jnp.bfloat16),
        compiler_params=pltpu.CompilerParams(
            dimension_semantics=("arbitrary",), vmem_limit_bytes=12 * 1024 * 1024
        ),
        cost_estimate=pl.CostEstimate(flops=1, bytes_accessed=1, transcendentals=0),
    )(left, right)


def columns_product(left, right, more=(), flops=1, far=False, tile=512):
    rows, count = left.shape
    width = right.shape[1]

    def body(left_ref, right_ref, *refs):
        total = trans_times(left_ref[...], right_ref[...])
        for ref in refs[:-1]:
            total = total + high(ref[...])
        refs[-1][...] = low(total)

    spec = pl.BlockSpec((count, tile), lambda i: (0, i))
    return pl.pallas_call(
        body,
        grid=(width // tile,),
        in_specs=[whole(left.shape), pl.BlockSpec((rows, tile), lambda i: (0, i))]
        + [spec] * len(more),
        out_specs=spec,
        out_shape=(pltpu.HBM if far else jax.ShapeDtypeStruct)((count, width), jnp.bfloat16),
        compiler_params=pltpu.CompilerParams(
            dimension_semantics=("arbitrary",), vmem_limit_bytes=14 * 1024 * 1024
        ),
        cost_estimate=pl.CostEstimate(flops=flops, bytes_accessed=1, transcendentals=0),
    )(left, right, *more)


def mixer_product(left, right, more, first, last, deep, flops, tile=512):
    rows, count = left.shape
    width = right.shape[1]
    wide = first.shape[0]
    share, parts = wide // deep, count // wide

    def body(left_ref, right_ref, first_ref, last_ref, *refs):
        total = trans_times(left_ref[...], right_ref[...])
        for ref in refs[:-1]:
            total = total + high(ref[...])
        total = low(total)
        for plane in range(deep):
            own = slice(plane * share, (plane + 1) * share)
            refs[-1][plane, 0] = first_ref[own, :]
            for k in range(parts):
                refs[-1][plane, 1 + k] = total[k * wide + own.start : k * wide + own.stop]
            refs[-1][plane, 1 + parts] = last_ref[own, :]

    def columns(size):
        return pl.BlockSpec((size, tile), lambda i: (0, i))

    return pl.pallas_call(
        body,
        grid=(width // tile,),
        in_specs=[whole(left.shape), columns(rows), columns(wide), columns(wide)]
        + [columns(count)] * len(more),
        out_specs=pl.BlockSpec((deep, 2 + parts, share, tile), lambda i: (0, 0, 0, i)),
        out_shape=pltpu.HBM((deep, 2 + parts, share, width), jnp.bfloat16),
        compiler_params=pltpu.CompilerParams(
            dimension_semantics=("arbitrary",), vmem_limit_bytes=16 * 1024 * 1024
        ),
        cost_estimate=pl.CostEstimate(flops=flops, bytes_accessed=1, transcendentals=0),
    )(left, right, first, last, *more)


def ffn_call(body, lefts, rights, slopes, count, tile=256):
    rows, units = lefts[0].shape[0], rights[0].shape[0]
    tile = min(tile, rows)
    spec = pl.BlockSpec((tile, units), lambda i: (i, 0))
    return pl.pallas_call(
        body,
        grid=(rows // tile,),
        in_specs=[pl.BlockSpec((tile, left.shape[1]), lambda i: (i, 0)) for left in lefts]
        + [whole(right.shape) for right in rights]
        + [spec] * len(slopes),
        out_specs=[spec] * count,
        out_shape=[jax.ShapeDtypeStruct((rows, units), jnp.bfloat16)] * count,
        compiler_params=pltpu.CompilerParams(
            dimension_semantics=("arbitrary",), vmem_limit_bytes=20 * 1024 * 1024
        ),
        cost_estimate=pl.CostEstimate(flops=1, bytes_accessed=1, transcendentals=0),
    )(*lefts, *rights, *slopes)


def ffn_ahead(normed, gate, up):
    def body(normed_ref, gate_ref, up_ref, hidden_ref, gate_slope_ref, up_slope_ref):
        pre = times_trans(normed_ref[...], gate_ref[...])
        value = times_trans(normed_ref[...], up_ref[...])
        sigma = jax.nn.sigmoid(pre)
        activated = pre * sigma
        hidden_ref[...] = low(activated * value)
        gate_slope_ref[...] = low(value * sigma * (1.0 + pre * (1.0 - sigma)))
        up_slope_ref[...] = low(activated)

    return ffn_call(body, [normed], [gate, up], [], 3)


def ffn_back(grad, down, gate_slope, up_slope):
    def body(grad_ref, down_ref, gate_slope_ref, up_slope_ref, gate_ref, up_ref):
        grad_hidden = times_trans(grad_ref[...], down_ref[...])
        gate_ref[...] = low(grad_hidden * high(gate_slope_ref[...]))
        up_ref[...] = low(grad_hidden * high(up_slope_ref[...]))

    return ffn_call(body, [grad], [down], [gate_slope, up_slope], 2)


class Order:
    def __init__(self):
        self.last = ()

    def __call__(self, *values):
        values = lax.optimization_barrier((values, self.last))[0]
        return values if len(values) > 1 else values[0]

    def did(self, *results):
        self.last = results

    def wait(self, *results):
        self.last = (*self.last, *results)


class Groups:
    def __init__(self, fsdp, tp, order):
        self.fsdp, self.tp, self.order = fsdp, tp, order
        self.deep = fsdp // 4
        self.columns = [[b + 4 * a for a in range(self.deep)] for b in range(4)]

    def along(self, value):
        pairs = [(i, (i + 4) % self.fsdp) for i in range(self.fsdp)]
        return lax.ppermute(value, "fsdp", pairs)

    def swap(self, value, bit):
        return lax.ppermute(value, "fsdp", [(i, i ^ bit) for i in range(self.fsdp)])

    def across(self, value, places):
        pairs = [(i, (i + places) % self.tp) for i in range(self.tp)]
        return lax.ppermute(value, "tp", pairs)

    def next_core(self, value):
        return lax.ppermute(value, "tp", [(i, i + 1) for i in range(self.tp - 1)])

    def last_core(self, value):
        return lax.ppermute(value, "tp", [(i + 1, i) for i in range(self.tp - 1)])

    def cores(self, value):
        value = self.order(value)
        return [value] + [self.across(value, j) for j in range(1, self.tp)]

    def sum_cores(self, sent):
        return [self.across(self.order(value), -j) for j, value in enumerate(sent, 1)]

    def sum_bits(self, value, bits):
        for bit in bits:
            value = value + self.swap(value, bit)
        return value

    def gather_ordered(self, value):
        return lax.all_gather(
            value, "fsdp", axis=0, tiled=True, axis_index_groups=self.columns
        )

    def reduce_ordered(self, value):
        return lax.psum_scatter(
            value, "fsdp", scatter_dimension=0, tiled=True, axis_index_groups=self.columns
        )

    def stack(self, value, bits):
        stack = value[None]
        for bit in bits:
            stack = jnp.concatenate([stack, self.swap(self.order(stack), bit)], 0)
        return stack


class Rows:
    def __init__(self, groups, rows):
        self.groups, self.rows = groups, groups.order(rows)
        self.one = groups.swap(self.rows, 1)
        self.two = groups.swap(self.rows, 2)

    def middle(self):
        half = self.rows.shape[0] // 2
        self.groups.order.wait(self.one, self.two)
        top, bottom = self.groups.order(self.two[:half], self.one[half:])
        self.top = self.groups.swap(top, 1)
        self.bottom = self.groups.swap(bottom, 2)

    def end(self):
        order = self.groups.order
        order.wait(self.top, self.bottom)
        return jnp.concatenate(
            order(self.rows, self.one, self.two, self.top, self.bottom), 0
        )


class Sums:
    def __init__(self, groups, blocks, late=False):
        self.groups, self.late, blocks = groups, late, groups.order(blocks)
        own, one, two, far = (
            (block[: block.shape[0] // 2], block[block.shape[0] // 2 :])
            for block in jnp.split(blocks, 4)
        )
        self.own, self.one, self.two = own, one, two
        self.far = groups.swap(far[0], 1), groups.swap(far[1], 2)
        if not late:
            self.direct = groups.swap(one[0], 1), groups.swap(two[1], 2)

    def middle(self):
        order, swap = self.groups.order, self.groups.swap
        order.wait(self.far)
        first, second = order(*self.far)
        second = low(high(self.one[1]) + high(second))
        first = low(high(self.two[0]) + high(first))
        if self.late:
            second = jnp.concatenate([self.one[0], second], 0)
            first = jnp.concatenate([first, self.two[1]], 0)
        order.did(first, second)
        first, second = order(first, second)
        self.summed = swap(second, 1), swap(first, 2)

    def end(self):
        order = self.groups.order
        if self.late:
            order.wait(self.summed)
            one, two = order(*self.summed)
            return high(jnp.concatenate(self.own, 0)) + high(one) + high(two)
        order.wait(self.direct, self.summed)
        (one_first, two_second), (one_second, two_first) = order(self.direct, self.summed)
        return jnp.concatenate(
            [
                high(self.own[0]) + high(one_first) + high(two_first),
                high(self.own[1]) + high(one_second) + high(two_second),
            ],
            0,
        )


def after(value, *before):
    return lax.optimization_barrier((value, *before))[0]


def rms_scale(value):
    return lax.rsqrt(jnp.mean(value * value, -1, keepdims=True) + EPS)


def norm_back(value, scale, gain, grad_norm):
    scaled = grad_norm * gain
    return scale * scaled - value * scale**3 * jnp.mean(scaled * value, -1, keepdims=True)


def shift_down(value, places, before):
    return jnp.concatenate([before[:, 2 - places :], value[:, :-places]], 1)


def shift_up(value, places, after):
    return jnp.concatenate([value[:, places:], after[:, :places]], 1)


def on_device(
    tokens,
    seg_ids,
    norm1_gain,
    in_weight,
    conv_weight,
    out_weight,
    norm2_gain,
    gate_weight,
    up_weight,
    down_weight,
    cotangent,
    fsdp,
    tp,
):
    order = Order()
    groups = Groups(fsdp, tp, order)
    deep = groups.deep
    micro_count, own_rows, width = tokens.shape
    rows = micro_count * own_rows
    share = in_weight.shape[2]
    hidden_share = gate_weight.shape[1]
    wide_share = deep * share
    segments = 4 * micro_count
    chip = lax.axis_index("fsdp")
    core = lax.axis_index("tp")

    plane_bits, column_bits, bit = (1, 2), [], 4
    while bit < fsdp:
        column_bits.append(bit)
        bit *= 2

    mixer_own = jnp.concatenate(
        [in_weight.transpose(1, 2, 0).reshape(3 * share, width), out_weight], 0
    )
    mixer_all = groups.gather_ordered(mixer_own)
    pair_own = jnp.concatenate([gate_weight.T, up_weight.T], 0)
    pair_all = groups.gather_ordered(after(pair_own, mixer_own))
    down_all = groups.gather_ordered(after(down_weight, pair_own))

    plane = chip // 4
    same = []
    for places in (1, 2):
        equal = (seg_ids[:, places:] == seg_ids[:, :-places]).astype(jnp.float32)
        equal = jnp.concatenate([jnp.zeros((micro_count, places), jnp.float32), equal], 1)
        same.append(lax.dynamic_slice_in_dim(equal, core * own_rows, own_rows, 1))
    tokens_own = tokens.reshape(rows, width)
    cot_own = cotangent.reshape(rows, width)
    token_rows = Rows(groups, tokens_own)
    gains = groups.stack(jnp.stack([norm1_gain, norm2_gain]), column_bits)
    order.wait(gains, pair_own)
    taps = groups.stack(conv_weight, column_bits)
    order.wait(taps)
    gains = groups.stack(gains, plane_bits[:1])
    same = groups.stack(jnp.stack(same), plane_bits[:1])
    token_rows.middle()
    order.wait(gains, same)
    gains = groups.stack(gains, plane_bits[1:])
    same = groups.stack(same, plane_bits[1:])
    order.wait(gains, same)
    tokens_all = token_rows.end()
    order.did(tokens_all)
    taps = taps[jnp.arange(deep) ^ plane].transpose(1, 0, 2).reshape(3, wide_share)
    taps = [high(tap) for tap in groups.cores(taps)]
    order.wait(taps)
    cot_rows = Rows(groups, cot_own)
    same = same.reshape(4, 2, micro_count, own_rows)
    mask_one = same[:, 0].reshape(segments, own_rows, 1)
    mask_two = same[:, 1].reshape(segments, own_rows, 1)
    gains = gains.reshape(4, deep, 2, -1).swapaxes(0, 1).reshape(fsdp, 2, -1)
    gains = gains[jnp.arange(fsdp) ^ chip].transpose(1, 0, 2).reshape(2, width)
    gain_one = high(gains[0])
    gain_two = high(gains[1])
    tokens_now, gain_now = order(tokens_all, gain_one)
    wide = high(tokens_now)
    scale_all = rms_scale(wide)
    normed = low(wide * scale_all * gain_now)
    order.did(normed)
    cot_rows.middle()
    order.wait(mixer_all)

    mixers = groups.cores(mixer_all)
    in_mats, out_mats, parts, gated_in = [], [], [], []
    for j in range(tp):
        if j:
            order.wait(mixers[j])
        mat = order(mixers[j]).reshape(deep, 4, share, width).transpose(1, 0, 2, 3)
        in_mats.append(mat[:3].reshape(3 * wide_share, width))
        out_mats.append(mat[3].reshape(wide_share, width))
        order.did(in_mats[-1], out_mats[-1])
        normed_now, mat = order(normed, in_mats[-1])
        projected = times_trans(normed_now, mat).reshape(segments, own_rows, 3 * wide_share)
        parts.append([projected[..., k * wide_share : (k + 1) * wide_share] for k in range(3)])
        gated_in.append(parts[-1][1] * parts[-1][2])
        order.did(parts[-1], gated_in[-1])
    ends = groups.next_core(order(jnp.stack([value[:, -2:] for value in gated_in])))
    order.wait(ends)
    parts, gated_in, ends = order(parts, gated_in, ends)
    before = [ends[(j - 1) % tp] for j in range(tp)]
    one_back = [mask_one * shift_down(v, 1, b) for v, b in zip(gated_in, before)]
    two_back = [mask_two * shift_down(v, 2, b) for v, b in zip(gated_in, before)]
    conv_out = [
        tap[0] * v + tap[1] * one + tap[2] * two
        for tap, v, one, two in zip(taps, gated_in, one_back, two_back)
    ]
    mixed = [low(part[0] * out).reshape(4 * rows, -1) for part, out in zip(parts, conv_out)]
    mixer_out = sum_of_products(mixed, out_mats)
    order.did(mixer_out)
    cot_all = cot_rows.end()
    order.wait(cot_all)
    mixer_sums = Sums(groups, mixer_out, True)
    mixer_sums.middle()
    mixer_sum = mixer_sums.end()
    mixer_sum, tokens_now = order(mixer_sum, tokens_own)
    tokens_f = high(tokens_own)
    resid = high(tokens_now) + mixer_sum

    scale_two = rms_scale(resid)
    normed_own = low(resid * scale_two * gain_two)
    order.did(normed_own)
    two_rows = Rows(groups, normed_own)
    two_rows.middle()
    order.wait(pair_all)
    pairs = groups.cores(pair_all)
    gate, up = [], []
    normed_two = two_rows.end()
    order.did(normed_two)
    hidden, gate_slope, up_slope, grad_gate, grad_up = [], [], [], [], []
    for j in range(tp):
        order.wait(pairs[j])
        pair = order(pairs[j]).reshape(deep, 2, hidden_share, width)
        gate.append(pair[:, 0].reshape(deep * hidden_share, width))
        up.append(pair[:, 1].reshape(deep * hidden_share, width))
        order.did(gate[j], up[j])
        found = ffn_ahead(*order(normed_two, gate[j], up[j]))
        order.did(*found)
        for kept, value in zip((hidden, gate_slope, up_slope), found):
            kept.append(value)

    def core_terms(left, right, flops=1):
        left, right = order(left, right)
        sent = [columns_product(value, right, (), flops) for value in left[1:]]
        order.did(sent)
        return groups.sum_cores(sent)

    def own_term(left, right, got, flops=1, far=True):
        order.wait(got)
        left, right, got = order(left, right, got)
        total = columns_product(left, right, got, flops, far)
        order.did(total)
        return total

    got = core_terms(hidden, cot_all)
    down_total = own_term(hidden[0], cot_all, got)
    order.wait(down_all)
    down_mats = groups.cores(down_all)
    down_grad = groups.reduce_ordered(order(down_total))
    for j in range(tp):
        if j:
            order.wait(down_mats[j])
        found = ffn_back(*order(cot_all, down_mats[j], gate_slope[j], up_slope[j]))
        order.did(*found)
        grad_gate.append(found[0])
        grad_up.append(found[1])
    back_two = sum_of_products(*order(grad_gate + grad_up, gate + up))
    order.did(back_two)
    two_sums = Sums(groups, back_two, True)
    gate_got = core_terms(grad_gate, normed_two)
    gate_total = own_term(grad_gate[0], normed_two, gate_got)
    two_sums.middle()
    up_got = core_terms(grad_up, normed_two)
    gate_grad = groups.reduce_ordered(order(gate_total))
    up_total = own_term(grad_up[0], normed_two, up_got)
    grad_normed_two = two_sums.end()
    order.wait(down_grad)
    up_grad = groups.reduce_ordered(order(up_total))
    grad_normed_two = order(grad_normed_two)
    resid_back = norm_back(resid, scale_two, gain_two, grad_normed_two)
    grad_resid = high(cot_own) + resid_back
    grad_low = low(grad_resid)
    order.did(grad_low)
    mixer_rows = Rows(groups, grad_low)
    norm_two_term = jnp.sum(grad_normed_two * resid * scale_two, 0)
    mixer_rows.middle()
    hidden_now, down_now = order(hidden, down_mats)
    ffn_out = sum_of_products(hidden_now, down_now)
    order.did(ffn_out, norm_two_term)
    ffn_sums = Sums(groups, ffn_out, True)
    grad_mixer = mixer_rows.end()
    order.did(grad_mixer)

    many = 10**11
    grad_now, mats_now = order(grad_mixer, out_mats)
    grad_mixed = [
        times_trans(grad_now, mat).reshape(segments, own_rows, -1) for mat in mats_now
    ]
    grad_conv = [value * part[0] for value, part in zip(grad_mixed, parts)]
    grad_b = [
        low(value * out).reshape(4 * rows, -1) for value, out in zip(grad_mixed, conv_out)
    ]
    masked_one = [mask_one * value for value in grad_conv]
    masked_two = [mask_two * value for value in grad_conv]
    edges = jnp.stack(
        [jnp.concatenate([one[:, :2], two[:, :2]], 0) for one, two in zip(masked_one, masked_two)]
    )
    order.did(grad_b, grad_conv, edges)
    starts = groups.last_core(order(edges))
    ffn_sums.middle()
    b_got = core_terms(grad_b, normed, many)
    out_got = core_terms(mixed, grad_mixer, many)
    order.wait(starts)
    grad_conv_now, masked_one, masked_two, starts = order(
        grad_conv, masked_one, masked_two, starts
    )
    after_edge = [starts[(j + 1) % tp] for j in range(tp)]
    grad_gated = [
        tap[0] * value
        + tap[1] * shift_up(one, 1, edge[:segments])
        + tap[2] * shift_up(two, 2, edge[segments:])
        for tap, value, one, two, edge in zip(
            taps, grad_conv_now, masked_one, masked_two, after_edge
        )
    ]
    grad_cx = [
        jnp.concatenate([low(gg * part[k]).reshape(4 * rows, -1) for k in (2, 1)], 1)
        for gg, part in zip(grad_gated, parts)
    ]
    order.did(grad_cx)
    cx_got = core_terms(grad_cx, normed, many)
    b_total = own_term(grad_b[0], normed, b_got, many, False)
    out_total = own_term(mixed[0], grad_mixer, out_got, many, False)
    order.wait(gate_grad)
    order.wait(cx_got)
    mixer_total = mixer_product(
        *order(grad_cx[0], normed, cx_got, b_total, out_total), deep, many
    ).reshape(4 * wide_share, width)
    order.did(mixer_total)
    order.wait(ffn_sums.summed)
    order.wait(up_grad)
    mixer_grad = groups.reduce_ordered(order(mixer_total))
    grads_now, mats_now = order(grad_b + grad_cx, in_mats)
    cuts = [(mat, start) for start in (0, wide_share) for mat in mats_now]
    back_one = sum_of_products(grads_now, cuts)
    order.did(back_one)
    one_rows = Sums(groups, back_one, True)
    back_now = order(back_one)
    norm_one_term = jnp.sum(high(back_now) * wide * scale_all, 0)
    conv_terms = [
        jnp.stack([jnp.sum(gc * value, (0, 1)) for value in (gi, one, two)])
        for gc, gi, one, two in zip(grad_conv, gated_in, one_back, two_back)
    ]
    small = [
        jnp.stack(
            [
                norm_one_term,
                norm_two_term,
                jnp.pad(term.reshape(-1), (0, width - 3 * wide_share)),
            ]
        )
        for term in conv_terms
    ]
    order.did(small)
    one_rows.middle()
    block_output = low(resid + ffn_sums.end())
    order.did(block_output)
    small = order(small)
    total = small[0]
    for j in range(1, tp):
        total = total + groups.across(small[j], -j)
    total = groups.sum_bits(total, column_bits)
    order.wait(total)
    grad_normed = one_rows.end()
    input_back = norm_back(tokens_f, rms_scale(tokens_f), gain_one, grad_normed)
    input_grad = low(grad_resid + input_back)
    order.did(input_grad)
    total = order(total)
    conv_total = lax.dynamic_slice_in_dim(
        total[2, : 3 * wide_share].reshape(3, wide_share), plane * share, share, 1
    )
    gain_sums = groups.sum_bits(total[:2], plane_bits)
    gate_grad, up_grad = order(gate_grad, up_grad)
    gate_grad, up_grad = high(gate_grad).T, high(up_grad).T
    order.did(gate_grad, up_grad)
    order.wait(gain_sums)
    order.wait(mixer_grad)
    mixer_grad = order(mixer_grad)
    in_grad = high(mixer_grad[: 3 * share]).reshape(3, share, width)
    out_grad = high(mixer_grad[3 * share :])
    gain_share = norm1_gain.shape[0]
    gain_grads = lax.dynamic_slice_in_dim(gain_sums, chip * gain_share, gain_share, 1)
    return (
        block_output.reshape(tokens.shape),
        input_grad.reshape(tokens.shape),
        gain_grads[0],
        in_grad.transpose(2, 0, 1),
        conv_total,
        out_grad,
        gain_grads[1],
        gate_grad,
        up_grad,
        high(down_grad),
    )


def solution(mesh):
    fsdp, tp = mesh.shape["fsdp"], mesh.shape["tp"]

    def body(*args):
        return on_device(*args, fsdp, tp)

    return jax.shard_map(
        body,
        mesh=mesh,
        in_specs=(
            P(None, ("fsdp", "tp"), None),
            P(None, "fsdp"),
            P("fsdp"),
            P(None, None, ("fsdp", "tp")),
            P(None, ("fsdp", "tp")),
            P(("fsdp", "tp"), None),
            P("fsdp"),
            P(None, ("fsdp", "tp")),
            P(None, ("fsdp", "tp")),
            P(("fsdp", "tp"), None),
            P(None, ("fsdp", "tp"), None),
        ),
        out_specs=(
            P(None, ("fsdp", "tp"), None),
            P(None, ("fsdp", "tp"), None),
            P("fsdp"),
            P(None, None, ("fsdp", "tp")),
            P(None, ("fsdp", "tp")),
            P(("fsdp", "tp"), None),
            P("fsdp"),
            P(None, ("fsdp", "tp")),
            P(None, ("fsdp", "tp")),
            P(("fsdp", "tp"), None),
        ),
        check_vma=False,
    )
```
